128 devices in a mesh: wide: 8 (over z, core), narrow: 16 (over x, y).
Axes of the slice: x: 4, y: 4, z: 4, core: 2. Of those that a mesh axis runs over, the one named last changes fastest.
Arguments:
- vectors: float32 [131072, 1024], P(('wide', 'narrow'))
- pivots: int32 [256], replicated, may hold values from 0 to 131071, as said below
- integrals: float32 [131072, 256], P(('wide', 'narrow')), as said below
- destination: int32 [131072], P(('wide', 'narrow')), may hold values from 0 to 131071, as said below
Outputs:
- new_vectors: float32 [131072, 256], P(('wide', 'narrow'))
The draws below stay inside these ranges and needn't reach their ends.
Inputs may be any that keep to these rules, and one draw needn't show every extreme that they name: `pivots`: 256 distinct pair rows, the first and the last pair row among them. Every pair row is the destination of exactly one slot. Rows 1024 * d to 1024 * (d + 1) - 1 belong to the device of index d along wide+narrow; of the slots of one device, at most 16 belong to the rows of one device, and some device sends exactly 16 to some device. `integrals`: the pivot block of the residual is symmetric and positive definite.
All inputs are finite; a program needn't handle non-finite values.
Results may differ from the reference program's by a relative error of at most 0.000084.
Values sent between devices are 32-bit elements; how exact they have to be, the bound alone decides.
A program may use at most 64 MiB of HBM per device.

```python
import math
import jax
import jax.numpy as jnp
from jax import lax

ROWS_DEV = 1024
VECS = 1024
PIVOTS = 256
PAIRS = 131072
CAP = 16


def pick_pivots(key):
    base_key = jax.random.fold_in(key, 101)
    subkeys = jax.random.split(base_key, 2)
    middle_rows = jax.random.permutation(subkeys[0], PAIRS - 2)[:PIVOTS - 2] + 1
    chosen = jnp.concatenate([jnp.array([0, PAIRS - 1], jnp.int32), middle_rows.astype(jnp.int32)])
    return jax.random.permutation(subkeys[1], chosen).astype(jnp.int32)


def route_rows(key):
    device_count = PAIRS // ROWS_DEV
    base_key = jax.random.fold_in(key, 202)
    subkeys = jax.random.split(base_key, 6)
    group_count = device_count // 2
    cut_points = jax.random.randint(subkeys[0], (group_count, 1), 0, CAP + 1).astype(jnp.int32)
    pieces = jnp.concatenate([cut_points, CAP - cut_points], axis=1)
    pieces = pieces.at[0].set(jnp.array([CAP, 0], jnp.int32))
    counts = jax.random.permutation(subkeys[1], pieces.reshape(-1))
    segment_ends = jnp.cumsum(counts)
    source_order = jax.random.permutation(subkeys[2], device_count).astype(jnp.int32)
    owner_shift = jax.random.permutation(subkeys[3], device_count).astype(jnp.int32)
    row_rotate = jax.random.randint(subkeys[4], (device_count, 1), 0, ROWS_DEV).astype(jnp.int32)
    local_rows = jnp.arange(ROWS_DEV, dtype=jnp.int32)[None, :]
    turned = (local_rows + row_rotate) % ROWS_DEV
    segment = jnp.sum((turned[:, :, None] >= segment_ends[None, None, :]).astype(jnp.int32), axis=2)
    sources = source_order[(segment - owner_shift[:, None]) % device_count]
    grouped = jnp.argsort(sources.reshape(-1), stable=True).astype(jnp.int32).reshape(device_count, ROWS_DEV)
    shuffle_keys = jax.random.split(subkeys[5], device_count)
    shuffles = jax.vmap(lambda one_key: jax.random.permutation(one_key, ROWS_DEV))(shuffle_keys)
    return jnp.take_along_axis(grouped, shuffles.astype(jnp.int32), axis=1).reshape(-1).astype(jnp.int32)


def draw_pivots(key, part):
    return pick_pivots(key)


def draw_destination(key, part):
    return route_rows(key)


def draw_vectors(key, part):
    own_key = jax.random.fold_in(key, 404)
    spread = 2.0 / math.sqrt(VECS)
    return jax.random.normal(own_key, (PAIRS, VECS), jnp.float32) * spread


def draw_integrals(key, part):
    pivots = pick_pivots(key)
    destination = route_rows(key)
    own_key = jax.random.fold_in(key, 303)
    subkeys = jax.random.split(own_key, 2)
    general = jax.random.normal(subkeys[0], (PAIRS, PIVOTS), jnp.float32)
    noise_part = jax.random.normal(subkeys[1], (PIVOTS, PIVOTS), jnp.float32) * (0.6 / math.sqrt(PIVOTS))
    pivot_block = noise_part + noise_part.T + 20.0 * jnp.eye(PIVOTS, dtype=jnp.float32)
    matches = (destination[:, None] == pivots[None, :]).astype(jnp.float32)
    pivot_values = jnp.dot(matches, pivot_block, precision=lax.Precision.HIGHEST)
    is_pivot = jnp.sum(matches, axis=1, keepdims=True)
    return jnp.where(is_pivot > 0.5, pivot_values, general)


def setup_inputs(seed: int = 0) -> dict:
    key_list = jax.random.split(jax.random.key(seed), 5)
    vectors = draw_vectors(jax.random.fold_in(key_list[4], 71), 0)
    pivots = draw_pivots(jax.random.fold_in(key_list[4], 71), 0)
    integrals = draw_integrals(jax.random.fold_in(key_list[4], 71), 0)
    destination = draw_destination(jax.random.fold_in(key_list[4], 71), 0)
    return {"vectors": vectors, "pivots": pivots, "integrals": integrals, "destination": destination}


def reference(vectors, pivots, integrals, destination):
    integral_matrix = jnp.zeros((PAIRS, PIVOTS), jnp.float32).at[destination].set(integrals)
    pivot_vectors = vectors[pivots]
    residual = integral_matrix - jnp.dot(vectors.astype(jnp.float32), pivot_vectors.T.astype(jnp.float32), precision=lax.Precision.HIGHEST, preferred_element_type=jnp.float32)
    pivot_block = residual[pivots]
    factor = jnp.linalg.cholesky(pivot_block)
    return jax.scipy.linalg.solve_triangular(factor, residual.T, lower=True).T
```

```python
import jax, jax.numpy as jnp
from jax import lax
from jax.experimental import pallas as pl
from jax.experimental.pallas import tpu as pltpu
from jax.sharding import Mesh
from jax.sharding import PartitionSpec as P

F32, BF16, I32 = jnp.float32, jnp.bfloat16, jnp.int32
HI = lax.Precision.HIGHEST
NT = (((1,), (1,)), ((), ()))
NN = (((1,), (0,)), ((), ()))
BLOCK = 64
PAIRS = 131072
ROWS_DEV = 1024
VECS = 1024
PIVOTS = 256
CAP = 16


def dot_hi(a, b, dims=(((1,), (0,)), ((), ()))):
    return lax.dot_general(a, b, dims, precision=HI, preferred_element_type=F32)

def factor_block(s, at):
    rows = lax.broadcasted_iota(I32, (BLOCK, 2 * BLOCK), 0)
    lanes = lax.broadcasted_iota(I32, (BLOCK, 2 * BLOCK), 1)
    other = BLOCK - at
    inside = (lanes >= at) & (lanes < at + BLOCK)
    t = jnp.where(inside, s, (rows == lanes - other).astype(F32))
    done = []
    for j in range(0, BLOCK, 2):
        top = j // 8 * 8
        i = j - top
        r0, r1 = t[i : i + 1, :], t[i + 1 : i + 2, :]
        c0 = jnp.broadcast_to(t[:, at + j : at + j + 1], t.shape)
        c1 = jnp.broadcast_to(t[:, at + j + 1 : at + j + 2], t.shape)
        a, b, c = c0[i : i + 1, :], c0[i + 1 : i + 2, :], c1[i + 1 : i + 2, :]
        inv = 1.0 / (a * c - b * b)
        u0 = (c * inv) * r0 - (b * inv) * r1
        u1 = (a * inv) * r1 - (b * inv) * r0
        ia = 1.0 / a
        done.append(r0 * lax.rsqrt(a))
        done.append((r1 - (b * ia) * r0) * lax.rsqrt(c - b * (b * ia)))
        below = lax.broadcasted_iota(I32, t.shape, 0) > i + 1
        t = jnp.where(below, t - c0 * u0 - c1 * u1, t)
        if (j + 2) % 8 == 0:
            t = t[8:, :]
    full = jnp.concatenate(done, axis=0)
    return full[:, other : other + BLOCK]

def invert_factor(a_ref, w_ref):
    n = a_ref.shape[0]
    w_ref[...] = jnp.zeros_like(w_ref)
    for k in range(0, n, BLOCK):
        e = k + BLOCK
        base = k // 128 * 128
        inv = factor_block(a_ref[k:e, base : base + 128], k - base)
        if k == 0:
            wk = inv
        else:
            wk = jnp.concatenate([dot_hi(inv, w_ref[k:e, :k]), inv], axis=1)
        w_ref[k:e, :e] = wk
        if e < n:
            col = dot_hi(a_ref[e:, k:e], inv, NT)
            a_ref[e:, e:] = a_ref[e:, e:] - dot_hi(col, col, NT)
            w_ref[e:, :e] = w_ref[e:, :e] - dot_hi(col, wk)


WIDE_NARROW = ("wide_0", "wide_1", "narrow_0", "narrow_1")
WIDE = ("wide_0", "wide_1")
NARROW = ("narrow_0", "narrow_1")


def in_blocks(shard, dim, peers):
    before, after = (shard.shape[:dim], shard.shape[dim + 1 :])
    return jnp.moveaxis(shard.reshape(*before, peers, -1, *after), dim, 0)


def joined_along(blocks, dim):
    blocks = jnp.moveaxis(blocks, 0, dim)
    lengths = blocks.shape
    return blocks.reshape(*lengths[:dim], lengths[dim] * lengths[dim + 1], *lengths[dim + 2 :])


def exchange_both(shard, axis, axes, splits, concats):
    sizes = [lax.axis_size(a) for a in axes]
    blocks = in_blocks(shard, splits[0], sizes[0])
    blocks = jnp.moveaxis(in_blocks(blocks, splits[1] + 1, sizes[1]), 0, 1)
    inside = blocks.shape[2:]
    blocks = blocks.reshape(-1, *inside)
    blocks = lax.all_to_all(blocks, axis, split_axis=0, concat_axis=0, tiled=True)
    blocks = joined_along(blocks.reshape(*sizes, *inside), concats[0] + 1)
    return joined_along(blocks, concats[1])


def rows_for(lines, peers):
    spare = -lines.shape[0] % peers
    if not spare:
        return lines
    return jnp.concatenate([lines, jnp.zeros((spare, *lines.shape[1:]), lines.dtype)])


def copy_for_each(shard, axis):
    peers = lax.axis_size(axis)
    return lax.all_to_all(
        jnp.broadcast_to(shard[None], (peers, *shard.shape)), axis, 0, 0, tiled=True
    )


def whole_of(shard, axes, dim):
    far, near = axes
    initial = copy_for_each(shard, far)
    blocks = jnp.swapaxes(copy_for_each(initial, near), 0, 1)
    return joined_along(blocks.reshape(-1, *shard.shape), dim)


def sum_at_owner(shard, axis, dim):
    peers = lax.axis_size(axis)
    blocks = lax.all_to_all(in_blocks(shard, dim, peers), axis, 0, 0, tiled=True)
    return jnp.sum(blocks, axis=0)


def sum_by_axis(shard, axes, dim):
    far, near = axes
    own = sum_at_owner(in_blocks(shard, dim, lax.axis_size(far)), near, dim + 1)
    return jnp.sum(lax.all_to_all(own, far, 0, 0, tiled=True), axis=0)


def sum_by_parts(shard, axes):
    padded = rows_for(shard, lax.axis_size(axes[0]) * lax.axis_size(axes[1]))
    whole = whole_of(sum_by_axis(padded, axes, 0), axes, 0)
    return lax.slice_in_dim(whole, 0, len(shard)).reshape(shard.shape)


def in_one(arrays, axis):
    ends = [0]
    for a in arrays:
        ends.append(ends[-1] + a.size)
    subtotal = sum_by_parts(jnp.concatenate([a.ravel() for a in arrays]), axis)
    return tuple((subtotal[b:e].reshape(a.shape) for a, b, e in zip(arrays, ends, ends[1:])))


def split3(x):
    hi = x.astype(BF16)
    rest = x - hi.astype(F32)
    mid = rest.astype(BF16)
    return hi, mid, (rest - mid.astype(F32)).astype(BF16)


def dot_bf(a, b, dims=NN):
    return lax.dot_general(a, b, dims, preferred_element_type=F32)


def column(row):
    return jnp.broadcast_to(row.astype(F32), (128, row.shape[1])).T.astype(I32)


def prep_kernel(
    first_ref, piv_smem, piv_ref, dest_ref, ints_ref, vec_hbm,
    send_ref, tgt_ref, pivots_ref,
    place_ref, place_smem, vec_ref, sem, vec_sem,
):
    devices = PAIRS // ROWS_DEV
    load = pltpu.make_async_copy(vec_hbm, vec_ref, vec_sem)
    load.start()
    dest = dest_ref[...]
    owner = dest // ROWS_DEV
    local = dest - owner * ROWS_DEV
    onehot = lax.broadcasted_iota(I32, (devices, ROWS_DEV), 0) == owner
    onehot_bf = onehot.astype(F32).astype(BF16)
    before = (
        lax.broadcasted_iota(I32, (128, 128), 0) < lax.broadcasted_iota(I32, (128, 128), 1)
    ).astype(F32).astype(BF16)
    ranks = []
    carry = jnp.zeros((devices, 1), F32)
    for i in range(0, ROWS_DEV, 128):
        part = onehot_bf[:, i : i + 128]
        hot = onehot[:, i : i + 128]
        count = dot_bf(part, before) + carry
        ranks.append(jnp.sum(jnp.where(hot, count, 0.0), axis=0, keepdims=True))
        carry = carry + jnp.sum(hot.astype(F32), axis=1, keepdims=True)
    rank = jnp.concatenate(ranks, axis=1).astype(I32)
    place_ref[...] = owner * CAP + rank
    to_smem = pltpu.make_async_copy(place_ref, place_smem, sem)
    to_smem.start()
    hit = lax.broadcasted_iota(I32, (CAP, ROWS_DEV), 0) == rank
    local1 = local + 1
    high = jnp.where(hit, local1 // 32, 0).astype(F32).astype(BF16)
    low = jnp.where(hit, local1 % 32, 0).astype(F32).astype(BF16)
    tgt_ref[...] = (dot_bf(onehot_bf, high, NT) * 32.0 + dot_bf(onehot_bf, low, NT)).astype(I32)

    piv_col = column(piv_ref[...])
    match = jnp.concatenate(
        [piv_col == dest[:, i : i + 128] for i in range(0, ROWS_DEV, 128)], axis=1
    ).astype(F32).astype(BF16)
    pivots_ref[:, VECS:] = sum(dot_bf(match, part) for part in split3(ints_ref[...]))

    to_smem.wait()

    def put(t, _):
        s = pl.multiple_of(t * 8, 8)
        for u in range(8):
            send_ref[pl.ds(place_smem[0, s + u], 1), :] = ints_ref[pl.ds(s + u, 1), :]
        return 0

    lax.fori_loop(0, ROWS_DEV // 8, put, 0)
    load.wait()
    pivots_ref[:, :VECS] = jnp.zeros((PIVOTS, VECS), F32)
    first = first_ref[0]

    def pick(j, _):
        row = piv_smem[j] - first

        @pl.when((row >= 0) & (row < ROWS_DEV))
        def _():
            pivots_ref[pl.ds(j, 1), :VECS] = vec_ref[pl.ds(row, 1), :]

        return 0

    lax.fori_loop(0, PIVOTS, pick, 0, unroll=4)


def prepare(vectors, pivots, integrals, destination, first_row):
    devices = PAIRS // ROWS_DEV
    vmem = pl.BlockSpec(memory_space=pltpu.VMEM)
    smem = pl.BlockSpec(memory_space=pltpu.SMEM)
    return pl.pallas_call(
        prep_kernel,
        out_shape=(
            jax.ShapeDtypeStruct((devices * CAP, PIVOTS), F32),
            jax.ShapeDtypeStruct((devices, CAP), I32),
            jax.ShapeDtypeStruct((PIVOTS, VECS + PIVOTS), F32),
        ),
        in_specs=[smem, smem, vmem, vmem, vmem, pl.BlockSpec(memory_space=pl.ANY)],
        out_specs=(vmem, vmem, vmem),
        scratch_shapes=[
            pltpu.VMEM((1, ROWS_DEV), I32),
            pltpu.SMEM((1, ROWS_DEV), I32),
            pltpu.VMEM((ROWS_DEV, VECS), F32),
            pltpu.SemaphoreType.DMA,
            pltpu.SemaphoreType.DMA,
        ],
        name="prepare",
    )(first_row.reshape(1), pivots, pivots.reshape(1, -1), destination.reshape(1, -1), integrals, vectors)


def factor_kernel(piv_ref, w_ref, a_ref):
    vecs = piv_ref[:, :VECS]
    block = piv_ref[:, VECS:] - dot_hi(vecs, vecs, NT)
    a_ref[...] = (block + block.T) * 0.5
    invert_factor(a_ref, w_ref)


def factor(pivot_rows):
    return pl.pallas_call(
        factor_kernel,
        out_shape=jax.ShapeDtypeStruct((PIVOTS, PIVOTS), F32),
        scratch_shapes=[pltpu.VMEM((PIVOTS, PIVOTS), F32)],
        name="factor",
    )(pivot_rows)


def dot3(a, b, dims):
    ah = a.astype(BF16)
    al = (a - ah.astype(F32)).astype(BF16)
    bh = b.astype(BF16)
    bl = (b - bh.astype(F32)).astype(BF16)
    return dot_bf(ah, bh, dims) + (dot_bf(ah, bl, dims) + dot_bf(al, bh, dims))


def finish_kernel(tgt_smem, recv_ref, vec_ref, piv_ref, w_ref, out_ref, rows_ref):
    devices = PAIRS // ROWS_DEV
    product = dot3(vec_ref[...], piv_ref[...], NT)

    def take(d, _):
        for k in range(CAP):
            rows_ref[pl.ds(tgt_smem[d, k], 1), :] = recv_ref[pl.ds(d * CAP + k, 1), :]
        return 0

    lax.fori_loop(0, devices, take, 0)
    out_ref[...] = dot3(rows_ref[1 : ROWS_DEV + 1, :] - product, w_ref[...], NT)


def finish(targets, received, vectors, pivot_vecs, inverse):
    vmem = pl.BlockSpec(memory_space=pltpu.VMEM)
    return pl.pallas_call(
        finish_kernel,
        out_shape=jax.ShapeDtypeStruct((ROWS_DEV, PIVOTS), F32),
        in_specs=[pl.BlockSpec(memory_space=pltpu.SMEM)] + [vmem] * 4,
        out_specs=vmem,
        scratch_shapes=[pltpu.VMEM((ROWS_DEV + 8, PIVOTS), F32)],
        name="finish",
    )(targets, received, vectors, pivot_vecs, inverse)


def shards(vectors, pivots, integrals, destination):
    first_row = lax.axis_index(WIDE_NARROW) * ROWS_DEV
    send_values, send_targets, own_pivots = prepare(vectors, pivots, integrals, destination, first_row)
    wide_count = lax.axis_size(WIDE)
    narrow_count = lax.axis_size(NARROW)
    values, targets = (
        exchange_both(
            send_values.reshape(wide_count, narrow_count, CAP, PIVOTS),
            WIDE_NARROW, (WIDE, NARROW), (0, 1), (0, 1),
        ),
        exchange_both(
            send_targets.reshape(wide_count, narrow_count, CAP),
            WIDE_NARROW, (WIDE, NARROW), (0, 1), (0, 1),
        ),
    )
    (pivot_rows,) = in_one((own_pivots,), (("wide_0", "wide_1", "narrow_0"), "narrow_1"))
    inverse = factor(pivot_rows)
    targets = targets.reshape(wide_count * narrow_count, CAP)
    return finish(targets, values.reshape(-1, PIVOTS), vectors, pivot_rows[:, :VECS], inverse)


def solution(mesh):
    torus = Mesh(mesh.devices.reshape(4, 2, 4, 4), ("wide_0", "wide_1", "narrow_0", "narrow_1"))
    return jax.shard_map(
        shards,
        mesh=torus,
        in_specs=(P(WIDE_NARROW, None), P(), P(WIDE_NARROW, None), P(WIDE_NARROW)),
        out_specs=P(WIDE_NARROW, None),
        check_vma=False,
    )
```

```python
import random

import jax, jax.numpy as jnp
from jax import lax
from jax.experimental import pallas as pl
from jax.experimental.pallas import tpu as pltpu
from jax.sharding import PartitionSpec as P

F32, BF16, I32 = jnp.float32, jnp.bfloat16, jnp.int32
HI = lax.Precision.HIGHEST
NT = (((1,), (1,)), ((), ()))
NN = (((1,), (0,)), ((), ()))
BLOCK = 64
PAIRS = 131072
ROWS_DEV = 1024
VECS = 1024
PIVOTS = 256
CAP = 16
DEVICES = PAIRS // ROWS_DEV
CHIPS = DEVICES // 2
WIDE_NARROW = ("wide", "narrow")


def dot_hi(a, b, dims=(((1,), (0,)), ((), ()))):
    return lax.dot_general(a, b, dims, precision=HI, preferred_element_type=F32)

def factor_block(s, at):
    rows = lax.broadcasted_iota(I32, (BLOCK, 2 * BLOCK), 0)
    lanes = lax.broadcasted_iota(I32, (BLOCK, 2 * BLOCK), 1)
    other = BLOCK - at
    inside = (lanes >= at) & (lanes < at + BLOCK)
    t = jnp.where(inside, s, (rows == lanes - other).astype(F32))
    done = []
    for j in range(0, BLOCK, 2):
        top = j // 8 * 8
        i = j - top
        r0, r1 = t[i : i + 1, :], t[i + 1 : i + 2, :]
        c0 = jnp.broadcast_to(t[:, at + j : at + j + 1], t.shape)
        c1 = jnp.broadcast_to(t[:, at + j + 1 : at + j + 2], t.shape)
        a, b, c = c0[i : i + 1, :], c0[i + 1 : i + 2, :], c1[i + 1 : i + 2, :]
        inv = 1.0 / (a * c - b * b)
        u0 = (c * inv) * r0 - (b * inv) * r1
        u1 = (a * inv) * r1 - (b * inv) * r0
        ia = 1.0 / a
        done.append(r0 * lax.rsqrt(a))
        done.append((r1 - (b * ia) * r0) * lax.rsqrt(c - b * (b * ia)))
        below = lax.broadcasted_iota(I32, t.shape, 0) > i + 1
        t = jnp.where(below, t - c0 * u0 - c1 * u1, t)
        if (j + 2) % 8 == 0:
            t = t[8:, :]
    full = jnp.concatenate(done, axis=0)
    return full[:, other : other + BLOCK]

def invert_factor(a_ref, w_ref):
    n = a_ref.shape[0]
    w_ref[...] = jnp.zeros_like(w_ref)
    for k in range(0, n, BLOCK):
        e = k + BLOCK
        base = k // 128 * 128
        inv = factor_block(a_ref[k:e, base : base + 128], k - base)
        if k == 0:
            wk = inv
        else:
            wk = jnp.concatenate([dot_hi(inv, w_ref[k:e, :k]), inv], axis=1)
        w_ref[k:e, :e] = wk
        if e < n:
            col = dot_hi(a_ref[e:, k:e], inv, NT)
            a_ref[e:, e:] = a_ref[e:, e:] - dot_hi(col, col, NT)
            w_ref[e:, :e] = w_ref[e:, :e] - dot_hi(col, wk)


def split3(x):
    hi = x.astype(BF16)
    rest = x - hi.astype(F32)
    mid = rest.astype(BF16)
    return hi, mid, (rest - mid.astype(F32)).astype(BF16)


def dot_bf(a, b, dims=NN):
    return lax.dot_general(a, b, dims, preferred_element_type=F32)


def dot3(a, b, dims):
    ah = a.astype(BF16)
    al = (a - ah.astype(F32)).astype(BF16)
    bh = b.astype(BF16)
    bl = (b - bh.astype(F32)).astype(BF16)
    return dot_bf(ah, bh, dims) + (dot_bf(ah, bl, dims) + dot_bf(al, bh, dims))


def column(row):
    return jnp.broadcast_to(row.astype(F32), (128, row.shape[1])).T.astype(I32)


def prep_kernel(
    first_ref, piv_smem, piv_ref, dest_ref, ints_ref, vec_hbm,
    send_ref, tgt_ref, pvec_ref, pint_ref,
    place_ref, place_smem, vec_ref, sem, vec_sem,
):
    load = pltpu.make_async_copy(vec_hbm, vec_ref, vec_sem)
    load.start()
    dest = dest_ref[...]
    owner = dest // ROWS_DEV
    local = dest - owner * ROWS_DEV
    onehot = lax.broadcasted_iota(I32, (DEVICES, ROWS_DEV), 0) == owner
    onehot_bf = onehot.astype(F32).astype(BF16)
    before = (
        lax.broadcasted_iota(I32, (128, 128), 0) < lax.broadcasted_iota(I32, (128, 128), 1)
    ).astype(F32).astype(BF16)
    ranks = []
    carry = jnp.zeros((DEVICES, 1), F32)
    for i in range(0, ROWS_DEV, 128):
        part = onehot_bf[:, i : i + 128]
        hot = onehot[:, i : i + 128]
        count = dot_bf(part, before) + carry
        ranks.append(jnp.sum(jnp.where(hot, count, 0.0), axis=0, keepdims=True))
        carry = carry + jnp.sum(hot.astype(F32), axis=1, keepdims=True)
    rank = jnp.concatenate(ranks, axis=1).astype(I32)
    place_ref[...] = owner * CAP + rank
    to_smem = pltpu.make_async_copy(place_ref, place_smem, sem)
    to_smem.start()
    hit = lax.broadcasted_iota(I32, (128, ROWS_DEV), 0) == rank
    local1 = local + 1
    high = jnp.where(hit, local1 // 32, 0).astype(F32).astype(BF16)
    low = jnp.where(hit, local1 % 32, 0).astype(F32).astype(BF16)
    target = (dot_bf(onehot_bf, high, NT) * 32.0 + dot_bf(onehot_bf, low, NT)).astype(I32)
    tgt_ref[...] = target.reshape(DEVICES, 1, 128)

    piv_col = column(piv_ref[...])
    match = jnp.concatenate(
        [piv_col == dest[:, i : i + 128] for i in range(0, ROWS_DEV, 128)], axis=1
    ).astype(F32).astype(BF16)
    rows = sum(dot_bf(match, part) for part in split3(ints_ref[...]))
    for ct in range(PIVOTS // 128):
        pint_ref[:, ct] = rows[:, ct * 128 : ct * 128 + 128].reshape(PIVOTS // 8, 8, 128)

    to_smem.wait()

    def put(t, _):
        s = pl.multiple_of(t * 8, 8)
        for u in range(8):
            send_ref[pl.ds(place_smem[0, s + u], 1), :] = ints_ref[pl.ds(s + u, 1), :]
        return 0

    lax.fori_loop(0, ROWS_DEV // 8, put, 0)
    load.wait()
    pvec_ref[...] = jnp.zeros(pvec_ref.shape, F32)
    first = first_ref[0]

    def pick(j, _):
        row = piv_smem[j] - first

        @pl.when((row >= 0) & (row < ROWS_DEV))
        def _():
            values = vec_ref[pl.ds(row, 1), :]
            for ct in range(VECS // 128):
                pvec_ref[j // 128, j % 128 // 8, ct // 2, ct % 2, pl.ds(j % 8, 1), :] = values[
                    :, ct * 128 : ct * 128 + 128
                ]

        return 0

    lax.fori_loop(0, PIVOTS, pick, 0)


def prepare(vectors, pivots, integrals, destination, first_row):
    vmem = pl.BlockSpec(memory_space=pltpu.VMEM)
    smem = pl.BlockSpec(memory_space=pltpu.SMEM)
    return pl.pallas_call(
        prep_kernel,
        out_shape=(
            jax.ShapeDtypeStruct((DEVICES * CAP, PIVOTS), F32),
            jax.ShapeDtypeStruct((DEVICES, 1, 128), I32),
            jax.ShapeDtypeStruct((2, 16, 4, 2, 8, 128), F32),
            jax.ShapeDtypeStruct((32, 2, 8, 128), F32),
        ),
        in_specs=[smem, smem, vmem, vmem, vmem, pl.BlockSpec(memory_space=pl.ANY)],
        out_specs=(vmem, vmem, vmem, vmem),
        scratch_shapes=[
            pltpu.VMEM((1, ROWS_DEV), I32),
            pltpu.SMEM((1, ROWS_DEV), I32),
            pltpu.VMEM((ROWS_DEV, VECS), F32),
            pltpu.SemaphoreType.DMA,
            pltpu.SemaphoreType.DMA,
        ],
        name="prepare",
    )(first_row.reshape(1), pivots, pivots.reshape(1, -1), destination.reshape(1, -1), integrals, vectors)


def far_first(offsets):
    offsets = list(offsets)
    random.Random(7).shuffle(offsets)
    return sorted(offsets, key=lambda o: -sum(min(v, 4 - v) for v in o[:3]))


CHIP_STEPS = far_first((z, x, y) for z in range(4) for x in range(4) for y in range(4) if (z, x, y) != (0, 0, 0))
ALL_STEPS = far_first(
    (z, x, y, c)
    for z in range(4) for x in range(4) for y in range(4) for c in range(2)
    if (z, x, y, c) != (0, 0, 0, 0)
)


def main_kernel(
    send_ref, tgt_ref, pvec_ref, pint_ref, vec_hbm,
    recv_ref, rtgt_ref, w_ref, prod_ref,
    pair_v, pair_i, mine_v, mine_i, part_v, part_i, tile_v, tile_i, all_v, all_i,
    vec_ref, a_ref, ssem, rsem, lsem,
):
    wide, narrow = lax.axis_index("wide"), lax.axis_index("narrow")
    z, core, x, y = wide // 2, wide % 2, narrow // 4, narrow % 4
    chip = z * 16 + x * 4 + y

    def at(dz, dx, dy, dc=0):
        oz, ox, oy, oc = (z + dz) % 4, (x + dx) % 4, (y + dy) % 4, (core + dc) % 2
        return {"wide": oz * 2 + oc, "narrow": ox * 4 + oy}, oz * 16 + ox * 4 + oy, oc

    def send(src, dst, stage, where):
        pltpu.make_async_remote_copy(
            src_ref=src, dst_ref=dst, send_sem=ssem.at[stage], recv_sem=rsem.at[stage],
            device_id=where, device_id_type=pl.DeviceIdType.MESH,
        ).start()

    def arrived(ref, stage):
        pltpu.make_async_copy(ref, ref, rsem.at[stage]).wait()

    def left(ref, stage):
        pltpu.make_async_copy(ref, ref, ssem.at[stage]).wait()

    load = pltpu.make_async_copy(vec_hbm, vec_ref, lsem.at[0])
    load.start()
    barrier = pltpu.get_barrier_semaphore()
    for step in ALL_STEPS:
        pl.semaphore_signal(barrier, inc=1, device_id=at(*step)[0], device_id_type=pl.DeviceIdType.MESH)
    pl.semaphore_wait(barrier, DEVICES - 1)

    sibling = at(0, 0, 0, 1)[0]

    def rows_out(begin, end):
        for i in range(begin, end):
            where, _, _ = at(*ALL_STEPS[i])
            dst = where["wide"] * 16 + where["narrow"]
            send(send_ref.at[dst], recv_ref.at[i], 8, where)
            send(tgt_ref.at[dst], rtgt_ref.at[i], 9, where)

    send(pvec_ref.at[1 - core], pair_v, 0, sibling)

    @pl.when(core == 1)
    def _():
        send(pint_ref, pair_i, 1, sibling)

    me = wide * 16 + narrow
    own = pltpu.make_async_copy(send_ref.at[me], recv_ref.at[DEVICES - 1], lsem.at[1])
    own.start()
    own_tgt = pltpu.make_async_copy(tgt_ref.at[me], rtgt_ref.at[DEVICES - 1], lsem.at[2])
    own_tgt.start()
    rows_out(0, SPLIT[0])
    arrived(pair_v, 0)
    mine_v[...] = pvec_ref[core] + pair_v[...]

    @pl.when(core == 0)
    def _():
        arrived(pair_i, 1)
        mine_i[...] = pint_ref[...] + pair_i[...]

    for i, step in enumerate(CHIP_STEPS):
        where, home, _ = at(*step)
        send(mine_v.at[home // 4, home % 4], part_v.at[i], 2, where)

    @pl.when(core == 0)
    def _():
        for i, step in enumerate(CHIP_STEPS):
            where, home, _ = at(*step)
            send(mine_i.at[home // 2, home % 2], part_i.at[i], 3, where)

    rows_out(SPLIT[0], SPLIT[1])
    arrived(part_v, 2)
    tile_v[...] = jnp.sum(part_v[...], axis=0) + mine_v[chip // 4, chip % 4]
    all_v[core, chip // 4, chip % 4] = tile_v[...]

    @pl.when(core == 0)
    def _():
        arrived(part_i, 3)
        tile_i[...] = jnp.sum(part_i[...], axis=0) + mine_i[chip // 2, chip % 2]
        all_i[chip // 2, chip % 2] = tile_i[...]

    for step in CHIP_STEPS:
        send(tile_v, all_v.at[core, chip // 4, chip % 4], 4, at(*step)[0])

    @pl.when(core == 0)
    def _():
        for step in CHIP_STEPS:
            send(tile_i, all_i.at[chip // 2, chip % 2], 5, at(*step)[0])

    rows_out(SPLIT[1], SPLIT[2])
    arrived(part_v, 4)
    send(all_v.at[core], all_v.at[core], 6, sibling)

    @pl.when(core == 0)
    def _():
        arrived(part_i, 5)
        send(all_i, all_i, 7, sibling)

    rows_out(SPLIT[2], DEVICES - 1)
    arrived(pair_v, 6)

    @pl.when(core == 1)
    def _():
        arrived(pair_i, 7)

    def pivot_columns(ct):
        return jnp.concatenate(
            [all_v[:, :, ct, u].reshape(PIVOTS, 128) for u in range(2)], axis=1
        )

    block = jnp.concatenate([all_i[:, u].reshape(PIVOTS, 128) for u in range(2)], axis=1)
    for ct in range(VECS // 256):
        cols = pivot_columns(ct)
        block = block - dot_hi(cols, cols, NT)
    a_ref[...] = (block + block.T) * 0.5
    invert_factor(a_ref, w_ref)
    load.wait()
    prod_ref[...] = sum(
        dot3(vec_ref[:, ct * 256 : ct * 256 + 256], pivot_columns(ct), NT) for ct in range(VECS // 256)
    )
    arrived(recv_ref.at[pl.ds(0, DEVICES - 1)], 8)
    arrived(rtgt_ref.at[pl.ds(0, DEVICES - 1)], 9)
    own.wait()
    own_tgt.wait()
    left(pair_v, 0)
    left(part_v, 2)
    left(part_v, 4)
    left(pair_v, 6)
    left(recv_ref.at[pl.ds(0, DEVICES - 1)], 8)
    left(rtgt_ref.at[pl.ds(0, DEVICES - 1)], 9)

    @pl.when(core == 1)
    def _():
        left(pair_i, 1)

    @pl.when(core == 0)
    def _():
        left(part_i, 3)
        left(part_i, 5)
        left(pair_i, 7)


SPLIT = (10, 40, 80)


def exchange(send_values, send_targets, pivot_vecs, pivot_ints, vectors):
    vmem = pl.BlockSpec(memory_space=pltpu.VMEM)
    hbm = pl.BlockSpec(memory_space=pl.ANY)
    return pl.pallas_call(
        main_kernel,
        out_shape=(
            jax.ShapeDtypeStruct((DEVICES, CAP, PIVOTS), F32),
            jax.ShapeDtypeStruct((DEVICES, 1, 128), I32),
            jax.ShapeDtypeStruct((PIVOTS, PIVOTS), F32),
            jax.ShapeDtypeStruct((ROWS_DEV, PIVOTS), F32),
        ),
        in_specs=[hbm, hbm, vmem, vmem, hbm],
        out_specs=(hbm, hbm, vmem, vmem),
        scratch_shapes=[
            pltpu.VMEM((16, 4, 2, 8, 128), F32),
            pltpu.VMEM((32, 2, 8, 128), F32),
            pltpu.VMEM((16, 4, 2, 8, 128), F32),
            pltpu.VMEM((32, 2, 8, 128), F32),
            pltpu.VMEM((CHIPS - 1, 2, 8, 128), F32),
            pltpu.VMEM((CHIPS - 1, 8, 128), F32),
            pltpu.VMEM((2, 8, 128), F32),
            pltpu.VMEM((8, 128), F32),
            pltpu.VMEM((2, 16, 4, 2, 8, 128), F32),
            pltpu.VMEM((32, 2, 8, 128), F32),
            pltpu.VMEM((ROWS_DEV, VECS), F32),
            pltpu.VMEM((PIVOTS, PIVOTS), F32),
            pltpu.SemaphoreType.DMA((10,)),
            pltpu.SemaphoreType.DMA((10,)),
            pltpu.SemaphoreType.DMA((3,)),
        ],
        compiler_params=pltpu.CompilerParams(collective_id=0, has_side_effects=True),
        name="exchange",
    )(send_values, send_targets, pivot_vecs, pivot_ints, vectors)


def finish_kernel(tgt_smem, recv_ref, prod_ref, w_ref, out_ref, rows_ref):
    def take(d, _):
        for k in range(CAP):
            rows_ref[pl.ds(tgt_smem[d, 0, k], 1), :] = recv_ref[d, pl.ds(k, 1), :]
        return 0

    lax.fori_loop(0, DEVICES, take, 0)
    out_ref[...] = dot3(rows_ref[1 : ROWS_DEV + 1, :] - prod_ref[...], w_ref[...], NT)


def finish(targets, received, product, inverse):
    vmem = pl.BlockSpec(memory_space=pltpu.VMEM)
    return pl.pallas_call(
        finish_kernel,
        out_shape=jax.ShapeDtypeStruct((ROWS_DEV, PIVOTS), F32),
        in_specs=[pl.BlockSpec(memory_space=pltpu.SMEM)] + [vmem] * 3,
        out_specs=vmem,
        scratch_shapes=[pltpu.VMEM((ROWS_DEV + 8, PIVOTS), F32)],
        name="finish",
    )(targets, received, product, inverse)


def shards(vectors, pivots, integrals, destination):
    first_row = lax.axis_index(WIDE_NARROW) * ROWS_DEV
    send_values, send_targets, pivot_vecs, pivot_ints = prepare(
        vectors, pivots, integrals, destination, first_row
    )
    received, targets, inverse, product = exchange(
        send_values.reshape(DEVICES, CAP, PIVOTS), send_targets, pivot_vecs, pivot_ints, vectors
    )
    return finish(targets, received, product, inverse)


def solution(mesh):
    return jax.shard_map(
        shards,
        mesh=mesh,
        in_specs=(P(WIDE_NARROW, None), P(), P(WIDE_NARROW, None), P(WIDE_NARROW)),
        out_specs=P(WIDE_NARROW, None),
        check_vma=False,
    )
```

```python
import random

import jax, jax.numpy as jnp
from jax import lax
from jax.experimental import pallas as pl
from jax.experimental.pallas import tpu as pltpu
from jax.sharding import PartitionSpec as P

F32, BF16, I32 = jnp.float32, jnp.bfloat16, jnp.int32
HI = lax.Precision.HIGHEST
NT = (((1,), (1,)), ((), ()))
NN = (((1,), (0,)), ((), ()))
TN = (((0,), (0,)), ((), ()))
BLOCK = 64
PAIRS = 131072
ROWS_DEV = 1024
VECS = 1024
PIVOTS = 256
CAP = 16
DEVICES = PAIRS // ROWS_DEV
CHIPS = DEVICES // 2
WIDE_NARROW = ("wide", "narrow")


def dot_hi(a, b, dims=(((1,), (0,)), ((), ()))):
    return lax.dot_general(a, b, dims, precision=HI, preferred_element_type=F32)

def factor_block(s, at):
    rows = lax.broadcasted_iota(I32, (BLOCK, 2 * BLOCK), 0)
    lanes = lax.broadcasted_iota(I32, (BLOCK, 2 * BLOCK), 1)
    other = BLOCK - at
    inside = (lanes >= at) & (lanes < at + BLOCK)
    t = jnp.where(inside, s, (rows == lanes - other).astype(F32))
    done = []
    for j in range(0, BLOCK, 2):
        top = j // 8 * 8
        i = j - top
        r0, r1 = t[i : i + 1, :], t[i + 1 : i + 2, :]
        c0 = jnp.broadcast_to(t[:, at + j : at + j + 1], t.shape)
        c1 = jnp.broadcast_to(t[:, at + j + 1 : at + j + 2], t.shape)
        a, b, c = c0[i : i + 1, :], c0[i + 1 : i + 2, :], c1[i + 1 : i + 2, :]
        inv = 1.0 / (a * c - b * b)
        u0 = (c * inv) * r0 - (b * inv) * r1
        u1 = (a * inv) * r1 - (b * inv) * r0
        ia = 1.0 / a
        done.append(r0 * lax.rsqrt(a))
        done.append((r1 - (b * ia) * r0) * lax.rsqrt(c - b * (b * ia)))
        below = lax.broadcasted_iota(I32, t.shape, 0) > i + 1
        t = jnp.where(below, t - c0 * u0 - c1 * u1, t)
        if (j + 2) % 8 == 0:
            t = t[8:, :]
    full = jnp.concatenate(done, axis=0)
    return full[:, other : other + BLOCK]

def invert_factor(a_ref, w_ref):
    n = a_ref.shape[0]
    w_ref[...] = jnp.zeros_like(w_ref)
    for k in range(0, n, BLOCK):
        e = k + BLOCK
        base = k // 128 * 128
        inv = factor_block(a_ref[k:e, base : base + 128], k - base)
        if k == 0:
            wk = inv
        else:
            wk = jnp.concatenate([dot_hi(inv, w_ref[k:e, :k]), inv], axis=1)
        w_ref[k:e, :e] = wk
        if e < n:
            col = dot_hi(a_ref[e:, k:e], inv, NT)
            a_ref[e:, e:] = a_ref[e:, e:] - dot_hi(col, col, NT)
            w_ref[e:, :e] = w_ref[e:, :e] - dot_hi(col, wk)


def dot_bf(a, b, dims=NN):
    return lax.dot_general(a, b, dims, preferred_element_type=F32)


def bf(x):
    return x.astype(F32).astype(BF16)


def split3(x):
    hi = x.astype(BF16)
    rest = x - hi.astype(F32)
    mid = rest.astype(BF16)
    return hi, mid, (rest - mid.astype(F32)).astype(BF16)


def dot3(a, b, dims):
    ah = a.astype(BF16)
    al = (a - ah.astype(F32)).astype(BF16)
    bh = b.astype(BF16)
    bl = (b - bh.astype(F32)).astype(BF16)
    return dot_bf(ah, bh, dims) + (dot_bf(ah, bl, dims) + dot_bf(al, bh, dims))


def column(row):
    return jnp.broadcast_to(row.astype(F32), (128, row.shape[1])).T.astype(I32)


def own_pivot_integrals(piv, dest, ints_ref, pint_ref):
    piv_col = column(piv)
    match = bf(
        jnp.concatenate([piv_col == dest[:, i : i + 128] for i in range(0, ROWS_DEV, 128)], axis=1)
    )
    rows = sum(dot_bf(match, part) for part in split3(ints_ref[...]))
    for ct in range(PIVOTS // 128):
        pint_ref[ct * 32 : ct * 32 + 32] = rows[:, ct * 128 : ct * 128 + 128].reshape(32, 8, 128)


def own_pivot_vectors(piv_smem, first, vec_ref, pvec_ref):
    def pick(t, _):
        for u in range(8):
            row = piv_smem[t * 8 + u] - first
            mine = (row >= 0) & (row < ROWS_DEV)
            values = vec_ref[pl.ds(jnp.where(mine, row, ROWS_DEV), 1), :]
            for ct in range(VECS // 128):
                pvec_ref[t // 16, ct // 2 * 16 + t % 16, ct % 2, u : u + 1, :] = values[
                    :, ct * 128 : ct * 128 + 128
                ]
        return 0

    lax.fori_loop(0, PIVOTS // 8, pick, 0)


def slot_maps(dest):
    owner = dest // ROWS_DEV
    local1 = dest - owner * ROWS_DEV + 1
    onehot = lax.broadcasted_iota(I32, (DEVICES, ROWS_DEV), 0) == owner
    onehot_bf = bf(onehot)
    before = bf(lax.broadcasted_iota(I32, (128, 128), 0) < lax.broadcasted_iota(I32, (128, 128), 1))
    ranks = []
    carry = jnp.zeros((DEVICES, 1), F32)
    for i in range(0, ROWS_DEV, 128):
        hot = onehot[:, i : i + 128]
        count = dot_bf(onehot_bf[:, i : i + 128], before) + carry
        ranks.append(jnp.sum(jnp.where(hot, count, 0.0), axis=0, keepdims=True))
        carry = carry + jnp.sum(hot.astype(F32), axis=1, keepdims=True)
    rank = jnp.concatenate(ranks, axis=1).astype(I32)
    slot = lax.broadcasted_iota(I32, (CAP, ROWS_DEV), 1)
    hit = lax.broadcasted_iota(I32, (CAP, ROWS_DEV), 0) == rank
    source = dot_bf(bf(jnp.where(hit, slot // 32, 0)), onehot_bf, NT) * 32.0
    source = source + dot_bf(bf(jnp.where(hit, slot % 32, 0)), onehot_bf, NT)
    hit = lax.broadcasted_iota(I32, (128, ROWS_DEV), 0) == rank
    target = dot_bf(onehot_bf, bf(jnp.where(hit, local1 // 32, 0)), NT) * 32.0
    target = target + dot_bf(onehot_bf, bf(jnp.where(hit, local1 % 32, 0)), NT)
    return jnp.clip(source.astype(I32), 0, ROWS_DEV - 1), target.astype(I32)


def row_places(target):
    by_slot = target.astype(F32).T.astype(I32)
    line = lax.broadcasted_iota(I32, (128, DEVICES), 0)
    block = lax.broadcasted_iota(I32, (128, DEVICES), 1)
    highs, blocks, slots = [], [], []
    for k in range(CAP):
        t = by_slot[k : k + 1, :] - 1
        highs.append(bf(line[:32] == t // 32))
        low = line == t % 32
        blocks.append(bf(jnp.where(low, block, 0)))
        slots.append(bf(jnp.where(low, k, 0)))
    high = jnp.concatenate(highs, axis=1)
    place = dot_bf(high, jnp.concatenate(blocks, axis=1), NT) * CAP
    place = place + dot_bf(high, jnp.concatenate(slots, axis=1), NT)
    return jnp.clip(place.astype(I32), 0, DEVICES * CAP - 1)


def far_first(offsets):
    offsets = list(offsets)
    random.Random(7).shuffle(offsets)
    return sorted(offsets, key=lambda o: -sum(min(v, 4 - v) for v in o[:3]))


CHIP_STEPS = far_first((z, x, y) for z in range(4) for x in range(4) for y in range(4) if (z, x, y) != (0, 0, 0))
ALL_STEPS = far_first(
    (z, x, y, c)
    for z in range(4) for x in range(4) for y in range(4) for c in range(2)
    if (z, x, y, c) != (0, 0, 0, 0)
)


def main_kernel(
    piv_smem, piv_ref, dest_ref, ints_hbm, vec_hbm, out_hbm,
    ints_ref, vec_ref, pvec_ref, pint_ref, from_ref, from_smem, send_ref, tgt_ref, rtgt_ref,
    pair_v, pair_i, mine, part, tile, all0, all1, a_ref, w_ref, prod_ref,
    recv_ref, place_ref, place_smem, rows_ref, out_ref, ssem, rsem, lsem, osem,
):
    wide, narrow = lax.axis_index("wide"), lax.axis_index("narrow")
    z, core, x, y = wide // 2, wide % 2, narrow // 4, narrow % 4
    chip = z * 16 + x * 4 + y
    me = wide * 16 + narrow

    def at(dz, dx, dy, dc=0):
        oz, ox, oy, oc = (z + dz) % 4, (x + dx) % 4, (y + dy) % 4, (core + dc) % 2
        return {"wide": oz * 2 + oc, "narrow": ox * 4 + oy}, oz * 16 + ox * 4 + oy

    def send(src, dst, stage, where):
        pltpu.make_async_remote_copy(
            src_ref=src, dst_ref=dst, send_sem=ssem.at[stage], recv_sem=rsem.at[stage],
            device_id=where, device_id_type=pl.DeviceIdType.MESH,
        ).start()

    def arrived(ref, stage):
        pltpu.make_async_copy(ref, ref, rsem.at[stage]).wait()

    def left(ref, stage):
        pltpu.make_async_copy(ref, ref, ssem.at[stage]).wait()

    load_vec = pltpu.make_async_copy(vec_hbm, vec_ref.at[pl.ds(0, ROWS_DEV)], lsem.at[0])
    load_vec.start()
    load_ints = pltpu.make_async_copy(ints_hbm, ints_ref, lsem.at[1])
    load_ints.start()
    barrier = pltpu.get_barrier_semaphore()
    for step in ALL_STEPS:
        pl.semaphore_signal(barrier, inc=1, device_id=at(*step)[0], device_id_type=pl.DeviceIdType.MESH)
    vec_ref[pl.ds(ROWS_DEV, 8), :] = jnp.zeros((8, VECS), F32)
    dest = dest_ref[...]
    load_ints.wait()
    own_pivot_integrals(piv_ref[...], dest, ints_ref, pint_ref)
    load_vec.wait()
    own_pivot_vectors(piv_smem, me * ROWS_DEV, vec_ref, pvec_ref)
    pl.semaphore_wait(barrier, DEVICES - 1)

    sibling = at(0, 0, 0, 1)[0]
    send(pvec_ref.at[1 - core], pair_v, 0, sibling)

    @pl.when(core == 1)
    def _():
        send(pint_ref, pair_i, 1, sibling)

    source, target = slot_maps(dest)
    from_ref[...] = source
    tgt_ref[...] = target.reshape(DEVICES, 1, 128)
    to_smem = pltpu.make_async_copy(from_ref, from_smem, lsem.at[2])
    to_smem.start()

    arrived(pair_v, 0)
    mine[:, 0:2] = pvec_ref[core] + pair_v[...]

    @pl.when(core == 0)
    def _():
        arrived(pair_i, 1)
        mine[:, 2] = pint_ref[...] + pair_i[...]
        for i, step in enumerate(CHIP_STEPS):
            where, home = at(*step)
            send(mine.at[home], part.at[i], 2, where)

    two = pl.ds(0, 2)

    @pl.when(core == 1)
    def _():
        for i, step in enumerate(CHIP_STEPS):
            where, home = at(*step)
            send(mine.at[home, two], part.at[i, two], 2, where)

    to_smem.wait()

    def pack(d, _):
        for k in range(CAP):
            send_ref[d, k : k + 1, :] = ints_ref[
                pl.ds(jnp.clip(from_smem[k, d], 0, ROWS_DEV - 1), 1), :
            ]
        return 0

    lax.fori_loop(0, DEVICES, pack, 0)
    others = pl.ds(0, CHIPS - 1)

    @pl.when(core == 0)
    def _():
        arrived(part, 2)
        tile[...] = jnp.sum(part[...], axis=0) + mine[chip]
        for step in CHIP_STEPS:
            send(tile, all0.at[chip], 4, at(*step)[0])
        all0[chip] = tile[...]

    @pl.when(core == 1)
    def _():
        arrived(all1.at[others], 2)
        tile[0:2] = jnp.sum(part[:, 0:2], axis=0) + mine[chip, 0:2]
        for step in CHIP_STEPS:
            send(tile.at[two], all1.at[chip], 4, at(*step)[0])
        all1[chip] = tile[0:2]

    steps = [at(*step)[0] for step in ALL_STEPS]
    for i, where in enumerate(steps):
        send(tgt_ref.at[where["wide"] * 16 + where["narrow"]], rtgt_ref.at[i], 9, where)
    rtgt_ref[DEVICES - 1] = tgt_ref[me]
    recv_ref[(DEVICES - 1) * CAP :, :] = send_ref[me]

    @pl.when(core == 0)
    def _():
        arrived(all0.at[others], 4)
        send(all0, all0, 6, sibling)

    @pl.when(core == 1)
    def _():
        arrived(all1.at[others], 4)
        send(all1, all1, 6, sibling)

    for i, where in enumerate(steps):
        send(
            send_ref.at[where["wide"] * 16 + where["narrow"]],
            recv_ref.at[pl.ds(i * CAP, CAP)], 8, where,
        )

    @pl.when(core == 0)
    def _():
        arrived(all1, 6)

    @pl.when(core == 1)
    def _():
        arrived(all0, 6)

    def pivot_columns(ct):
        top, end = ct * 16, ct * 16 + 16
        return jnp.concatenate(
            [
                jnp.concatenate(
                    [all0[top:end, u].reshape(128, 128), all1[top:end, u].reshape(128, 128)], axis=0
                )
                for u in range(2)
            ],
            axis=1,
        )

    block = jnp.concatenate([all0[u * 32 : u * 32 + 32, 2].reshape(PIVOTS, 128) for u in range(2)], axis=1)
    for ct in range(VECS // 256):
        cols = pivot_columns(ct)
        block = block - dot_hi(cols, cols, NT)
    a_ref[...] = (block + block.T) * 0.5
    invert_factor(a_ref, w_ref)
    prod_ref[...] = sum(
        dot3(vec_ref[:ROWS_DEV, ct * 256 : ct * 256 + 256], pivot_columns(ct), NT)
        for ct in range(VECS // 256)
    )
    arrived(rtgt_ref.at[pl.ds(0, DEVICES - 1)], 9)
    place_ref[...] = row_places(rtgt_ref[...].reshape(DEVICES, 128))
    place_copy = pltpu.make_async_copy(place_ref, place_smem, lsem.at[3])
    place_copy.start()
    place_copy.wait()
    arrived(recv_ref.at[pl.ds(0, (DEVICES - 1) * CAP)], 8)
    outs = []
    for q in range(4):
        top = q * 256

        def take(t, _, q=q):
            for u in range(32):
                place = jnp.clip(place_smem[q * 8 + t, u], 0, DEVICES * CAP - 1)
                rows_ref[t * 4 + u // 8, u % 8 : u % 8 + 1, :] = recv_ref[pl.ds(place, 1), :]
            return 0

        lax.fori_loop(0, 8, take, 0)
        residual = rows_ref[...].reshape(256, PIVOTS) - prod_ref[top : top + 256, :]
        out_ref[top : top + 256, :] = dot3(residual, w_ref[...], NT)
        out = pltpu.make_async_copy(
            out_ref.at[pl.ds(top, 256)], out_hbm.at[pl.ds(top, 256)], osem.at[q]
        )
        out.start()
        outs.append(out)

    left(pair_v, 0)
    left(recv_ref.at[pl.ds(0, (DEVICES - 1) * CAP)], 8)
    left(rtgt_ref.at[pl.ds(0, DEVICES - 1)], 9)

    @pl.when(core == 0)
    def _():
        left(part, 2)
        left(all0.at[others], 4)
        left(all0, 6)

    @pl.when(core == 1)
    def _():
        left(pair_i, 1)
        left(all1.at[others], 2)
        left(all1.at[others], 4)
        left(all1, 6)

    for out in outs:
        out.wait()


def exchange(vectors, pivots, integrals, destination):
    vmem = pl.BlockSpec(memory_space=pltpu.VMEM)
    hbm = pl.BlockSpec(memory_space=pl.ANY)
    return pl.pallas_call(
        main_kernel,
        out_shape=jax.ShapeDtypeStruct((ROWS_DEV, PIVOTS), F32),
        in_specs=[pl.BlockSpec(memory_space=pltpu.SMEM), vmem, vmem, hbm, hbm],
        out_specs=hbm,
        scratch_shapes=[
            pltpu.VMEM((ROWS_DEV, PIVOTS), F32),
            pltpu.VMEM((ROWS_DEV + 8, VECS), F32),
            pltpu.VMEM((2, CHIPS, 2, 8, 128), F32),
            pltpu.VMEM((CHIPS, 8, 128), F32),
            pltpu.VMEM((CAP, DEVICES), I32),
            pltpu.SMEM((CAP, DEVICES), I32),
            pltpu.VMEM((DEVICES, CAP, PIVOTS), F32),
            pltpu.VMEM((DEVICES, 1, 128), I32),
            pltpu.VMEM((DEVICES, 1, 128), I32),
            pltpu.VMEM((CHIPS, 2, 8, 128), F32),
            pltpu.VMEM((CHIPS, 8, 128), F32),
            pltpu.VMEM((CHIPS, 3, 8, 128), F32),
            pltpu.VMEM((CHIPS - 1, 3, 8, 128), F32),
            pltpu.VMEM((3, 8, 128), F32),
            pltpu.VMEM((CHIPS, 3, 8, 128), F32),
            pltpu.VMEM((CHIPS, 2, 8, 128), F32),
            pltpu.VMEM((PIVOTS, PIVOTS), F32),
            pltpu.VMEM((PIVOTS, PIVOTS), F32),
            pltpu.VMEM((ROWS_DEV, PIVOTS), F32),
            pltpu.VMEM((DEVICES * CAP, PIVOTS), F32),
            pltpu.VMEM((32, 128), I32),
            pltpu.SMEM((32, 128), I32),
            pltpu.VMEM((32, 8, PIVOTS), F32),
            pltpu.VMEM((ROWS_DEV, PIVOTS), F32),
            pltpu.SemaphoreType.DMA((10,)),
            pltpu.SemaphoreType.DMA((10,)),
            pltpu.SemaphoreType.DMA((4,)),
            pltpu.SemaphoreType.DMA((4,)),
        ],
        compiler_params=pltpu.CompilerParams(collective_id=0, has_side_effects=True),
        name="exchange",
    )(pivots, pivots.reshape(1, -1), destination.reshape(1, -1), integrals, vectors)


def solution(mesh):
    return jax.shard_map(
        exchange,
        mesh=mesh,
        in_specs=(P(WIDE_NARROW, None), P(), P(WIDE_NARROW, None), P(WIDE_NARROW)),
        out_specs=P(WIDE_NARROW, None),
        check_vma=False,
    )
```

```python
import random

import jax, jax.numpy as jnp
from jax import lax
from jax.experimental import pallas as pl
from jax.experimental.pallas import tpu as pltpu
from jax.sharding import PartitionSpec as P

F32, BF16, I32 = jnp.float32, jnp.bfloat16, jnp.int32
HI = lax.Precision.HIGHEST
NT = (((1,), (1,)), ((), ()))
NN = (((1,), (0,)), ((), ()))
TN = (((0,), (0,)), ((), ()))
BLOCK = 64
PAIRS = 131072
ROWS_DEV = 1024
VECS = 1024
PIVOTS = 256
CAP = 16
DEVICES = PAIRS // ROWS_DEV
CHIPS = DEVICES // 2
WIDE_NARROW = ("wide", "narrow")


def dot_hi(a, b, dims=(((1,), (0,)), ((), ()))):
    return lax.dot_general(a, b, dims, precision=HI, preferred_element_type=F32)

def factor_block(s, at):
    rows = lax.broadcasted_iota(I32, (BLOCK, 2 * BLOCK), 0)
    lanes = lax.broadcasted_iota(I32, (BLOCK, 2 * BLOCK), 1)
    other = BLOCK - at
    inside = (lanes >= at) & (lanes < at + BLOCK)
    t = jnp.where(inside, s, (rows == lanes - other).astype(F32))
    done = []
    for j in range(0, BLOCK, 2):
        top = j // 8 * 8
        i = j - top
        r0, r1 = t[i : i + 1, :], t[i + 1 : i + 2, :]
        c0 = jnp.broadcast_to(t[:, at + j : at + j + 1], t.shape)
        c1 = jnp.broadcast_to(t[:, at + j + 1 : at + j + 2], t.shape)
        a, b, c = c0[i : i + 1, :], c0[i + 1 : i + 2, :], c1[i + 1 : i + 2, :]
        inv = 1.0 / (a * c - b * b)
        u0 = (c * inv) * r0 - (b * inv) * r1
        u1 = (a * inv) * r1 - (b * inv) * r0
        ia = 1.0 / a
        done.append(r0 * lax.rsqrt(a))
        done.append((r1 - (b * ia) * r0) * lax.rsqrt(c - b * (b * ia)))
        below = lax.broadcasted_iota(I32, t.shape, 0) > i + 1
        t = jnp.where(below, t - c0 * u0 - c1 * u1, t)
        if (j + 2) % 8 == 0:
            t = t[8:, :]
    full = jnp.concatenate(done, axis=0)
    return full[:, other : other + BLOCK]

def invert_factor(a_ref, w_ref):
    n = a_ref.shape[0]
    w_ref[...] = jnp.zeros_like(w_ref)
    for k in range(0, n, BLOCK):
        e = k + BLOCK
        base = k // 128 * 128
        inv = factor_block(a_ref[k:e, base : base + 128], k - base)
        if k == 0:
            wk = inv
        else:
            wk = jnp.concatenate([dot_hi(inv, w_ref[k:e, :k]), inv], axis=1)
        w_ref[k:e, :e] = wk
        if e < n:
            col = dot_hi(a_ref[e:, k:e], inv, NT)
            a_ref[e:, e:] = a_ref[e:, e:] - dot_hi(col, col, NT)
            w_ref[e:, :e] = w_ref[e:, :e] - dot_hi(col, wk)


def dot_bf(a, b, dims=NN):
    return lax.dot_general(a, b, dims, preferred_element_type=F32)


def bf(x):
    return x.astype(F32).astype(BF16)


def split3(x):
    hi = x.astype(BF16)
    rest = x - hi.astype(F32)
    mid = rest.astype(BF16)
    return hi, mid, (rest - mid.astype(F32)).astype(BF16)


def dot3(a, b, dims):
    ah = a.astype(BF16)
    al = (a - ah.astype(F32)).astype(BF16)
    bh = b.astype(BF16)
    bl = (b - bh.astype(F32)).astype(BF16)
    return dot_bf(ah, bh, dims) + (dot_bf(ah, bl, dims) + dot_bf(al, bh, dims))


def column(row):
    return jnp.broadcast_to(row.astype(F32), (128, row.shape[1])).T.astype(I32)


def own_pivot_integrals(piv, dest, ints_ref, pint_ref):
    piv_col = column(piv)
    match = bf(
        jnp.concatenate([piv_col == dest[:, i : i + 128] for i in range(0, ROWS_DEV, 128)], axis=1)
    )
    rows = sum(dot_bf(match, part) for part in split3(ints_ref[...]))
    for ct in range(PIVOTS // 128):
        pint_ref[ct * 32 : ct * 32 + 32] = rows[:, ct * 128 : ct * 128 + 128].reshape(32, 8, 128)


def own_pivot_vectors(piv_smem, first, vec_ref, pvec_ref):
    def pick(t, _):
        for u in range(8):
            row = piv_smem[t * 8 + u] - first
            mine = (row >= 0) & (row < ROWS_DEV)
            values = vec_ref[pl.ds(jnp.where(mine, row, ROWS_DEV), 1), :]
            for ct in range(VECS // 128):
                pvec_ref[t // 16, ct // 2 * 16 + t % 16, ct % 2, u : u + 1, :] = values[
                    :, ct * 128 : ct * 128 + 128
                ]
        return 0

    lax.fori_loop(0, PIVOTS // 8, pick, 0)


def slot_maps(dest):
    owner = dest // ROWS_DEV
    local1 = dest - owner * ROWS_DEV + 1
    onehot = lax.broadcasted_iota(I32, (DEVICES, ROWS_DEV), 0) == owner
    onehot_bf = bf(onehot)
    before = bf(lax.broadcasted_iota(I32, (128, 128), 0) < lax.broadcasted_iota(I32, (128, 128), 1))
    ranks = []
    carry = jnp.zeros((DEVICES, 1), F32)
    for i in range(0, ROWS_DEV, 128):
        hot = onehot[:, i : i + 128]
        count = dot_bf(onehot_bf[:, i : i + 128], before) + carry
        ranks.append(jnp.sum(jnp.where(hot, count, 0.0), axis=0, keepdims=True))
        carry = carry + jnp.sum(hot.astype(F32), axis=1, keepdims=True)
    rank = jnp.concatenate(ranks, axis=1).astype(I32)
    slot = lax.broadcasted_iota(I32, (CAP, ROWS_DEV), 1)
    hit = lax.broadcasted_iota(I32, (CAP, ROWS_DEV), 0) == rank
    source = dot_bf(bf(jnp.where(hit, slot // 32, 0)), onehot_bf, NT) * 32.0
    source = source + dot_bf(bf(jnp.where(hit, slot % 32, 0)), onehot_bf, NT)
    hit = lax.broadcasted_iota(I32, (128, ROWS_DEV), 0) == rank
    target = dot_bf(onehot_bf, bf(jnp.where(hit, local1 // 32, 0)), NT) * 32.0
    target = target + dot_bf(onehot_bf, bf(jnp.where(hit, local1 % 32, 0)), NT)
    return jnp.clip(source.astype(I32), 0, ROWS_DEV - 1), target.astype(I32)


def row_places(target):
    by_slot = target.astype(F32).T.astype(I32)
    line = lax.broadcasted_iota(I32, (128, DEVICES), 0)
    block = lax.broadcasted_iota(I32, (128, DEVICES), 1)
    highs, blocks, slots = [], [], []
    for k in range(CAP):
        t = by_slot[k : k + 1, :] - 1
        highs.append(bf(line[:32] == t // 32))
        low = line == t % 32
        blocks.append(bf(jnp.where(low, block, 0)))
        slots.append(bf(jnp.where(low, k, 0)))
    high = jnp.concatenate(highs, axis=1)
    place = dot_bf(high, jnp.concatenate(blocks, axis=1), NT) * CAP
    place = place + dot_bf(high, jnp.concatenate(slots, axis=1), NT)
    place = place.astype(I32)
    return place // 8 * 16 + place % 8


def far_first(offsets):
    offsets = list(offsets)
    random.Random(7).shuffle(offsets)
    return sorted(offsets, key=lambda o: -sum(min(v, 4 - v) for v in o[:3]))


CHIP_STEPS = far_first((z, x, y) for z in range(4) for x in range(4) for y in range(4) if (z, x, y) != (0, 0, 0))
PLANE_ORDER = (2, 1, 3, 0)
ALL_STEPS = far_first(
    (z, x, y, c)
    for z in range(4) for x in range(4) for y in range(4) for c in range(2)
    if (z, x, y, c) != (0, 0, 0, 0)
)


def main_kernel(
    piv_smem, piv_ref, dest_ref, ints_hbm, vec_hbm, out_ref,
    ints_ref, vec_ref, pvec_ref, pint_ref, from_ref, from_smem, send_ref, tgt_ref, rtgt_ref,
    pair_v, pair_i, mine, part, tile, all0, all1, a_ref, w_ref, prod_ref,
    recv_ref, place_ref, place_smem, rows_ref, ssem, rsem, lsem,
):
    wide, narrow = lax.axis_index("wide"), lax.axis_index("narrow")
    z, core, x, y = wide // 2, wide % 2, narrow // 4, narrow % 4
    chip = z * 16 + x * 4 + y
    me = wide * 16 + narrow

    def at(dz, dx, dy, dc=0):
        oz, ox, oy, oc = (z + dz) % 4, (x + dx) % 4, (y + dy) % 4, (core + dc) % 2
        return {"wide": oz * 2 + oc, "narrow": ox * 4 + oy}, oz * 16 + ox * 4 + oy

    def send(src, dst, stage, where):
        pltpu.make_async_remote_copy(
            src_ref=src, dst_ref=dst, send_sem=ssem.at[stage], recv_sem=rsem.at[stage],
            device_id=where, device_id_type=pl.DeviceIdType.MESH,
        ).start()

    def arrived(ref, stage):
        pltpu.make_async_copy(ref, ref, rsem.at[stage]).wait()

    def left(ref, stage):
        pltpu.make_async_copy(ref, ref, ssem.at[stage]).wait()

    load_vec = pltpu.make_async_copy(vec_hbm, vec_ref.at[pl.ds(0, ROWS_DEV)], lsem.at[0])
    load_vec.start()
    load_ints = pltpu.make_async_copy(ints_hbm, ints_ref, lsem.at[1])
    load_ints.start()
    barrier = pltpu.get_barrier_semaphore()
    for step in ALL_STEPS:
        pl.semaphore_signal(barrier, inc=1, device_id=at(*step)[0], device_id_type=pl.DeviceIdType.MESH)
    vec_ref[pl.ds(ROWS_DEV, 8), :] = jnp.zeros((8, VECS), F32)
    dest = dest_ref[...]
    load_ints.wait()
    own_pivot_integrals(piv_ref[...], dest, ints_ref, pint_ref)
    load_vec.wait()
    own_pivot_vectors(piv_smem, me * ROWS_DEV, vec_ref, pvec_ref)
    pl.semaphore_wait(barrier, DEVICES - 1)

    sibling = at(0, 0, 0, 1)[0]
    planes = [pl.ds(pl.multiple_of((z + dz) % 4 * 16, 16), 16) for dz in PLANE_ORDER]
    for n, plane in enumerate(planes):
        send(pvec_ref.at[1 - core, plane], pair_v.at[plane], 10 + n, sibling)

        @pl.when(core == 1)
        def _():
            send(pint_ref.at[plane], pair_i.at[plane], 14 + n, sibling)

    source, target = slot_maps(dest)
    from_ref[...] = source
    tgt_ref[...] = target.reshape(DEVICES, 1, 128)
    to_smem = pltpu.make_async_copy(from_ref, from_smem, lsem.at[2])
    to_smem.start()

    two = pl.ds(0, 2)
    step_slot = {step: i for i, step in enumerate(CHIP_STEPS)}
    for n, plane in enumerate(planes):
        arrived(pair_v.at[plane], 10 + n)
        mine[plane, 0:2] = pvec_ref[core, plane] + pair_v[plane]
        group = [step for step in CHIP_STEPS if step[0] == PLANE_ORDER[n]]

        @pl.when(core == 0)
        def _():
            arrived(pair_i.at[plane], 14 + n)
            mine[plane, 2] = pint_ref[plane] + pair_i[plane]
            for step in group:
                where, home = at(*step)
                send(mine.at[home], part.at[step_slot[step]], 2, where)

        @pl.when(core == 1)
        def _():
            for step in group:
                where, home = at(*step)
                send(mine.at[home, two], part.at[step_slot[step], two], 2, where)

    to_smem.wait()

    def pack(d, _):
        for k in range(CAP):
            row = ints_ref[pl.ds(from_smem[k, d] & (ROWS_DEV - 1), 1), :]
            send_ref[d, pl.ds(k // 8 * 16 + k % 8, 2, 8), :] = jnp.concatenate(
                [row[:, :128], row[:, 128:]], axis=0
            )
        return 0

    lax.fori_loop(0, DEVICES, pack, 0)
    others = pl.ds(0, CHIPS - 1)

    @pl.when(core == 0)
    def _():
        arrived(part, 2)
        tile[...] = jnp.sum(part[...], axis=0) + mine[chip]
        for step in CHIP_STEPS:
            send(tile, all0.at[chip], 4, at(*step)[0])
        all0[chip] = tile[...]

    @pl.when(core == 1)
    def _():
        arrived(all1.at[others], 2)
        tile[0:2] = jnp.sum(part[:, 0:2], axis=0) + mine[chip, 0:2]
        for step in CHIP_STEPS:
            send(tile.at[two], all1.at[chip], 4, at(*step)[0])
        all1[chip] = tile[0:2]

    steps = [at(*step)[0] for step in ALL_STEPS]
    for i, where in enumerate(steps):
        send(tgt_ref.at[where["wide"] * 16 + where["narrow"]], rtgt_ref.at[i], 9, where)
    rtgt_ref[DEVICES - 1] = tgt_ref[me]
    recv_ref[2 * (DEVICES - 1) * CAP :, :] = send_ref[me]

    @pl.when(core == 0)
    def _():
        arrived(all0.at[others], 4)
        send(all0, all0, 6, sibling)

    @pl.when(core == 1)
    def _():
        arrived(all1.at[others], 4)
        send(all1, all1, 6, sibling)

    for i, where in enumerate(steps):
        send(
            send_ref.at[where["wide"] * 16 + where["narrow"]],
            recv_ref.at[pl.ds(2 * i * CAP, 2 * CAP)], 8, where,
        )

    @pl.when(core == 0)
    def _():
        arrived(all1, 6)

    @pl.when(core == 1)
    def _():
        arrived(all0, 6)

    def pivot_columns(ct):
        top, end = ct * 16, ct * 16 + 16
        return jnp.concatenate(
            [
                jnp.concatenate(
                    [all0[top:end, u].reshape(128, 128), all1[top:end, u].reshape(128, 128)], axis=0
                )
                for u in range(2)
            ],
            axis=1,
        )

    block = jnp.concatenate([all0[u * 32 : u * 32 + 32, 2].reshape(PIVOTS, 128) for u in range(2)], axis=1)
    for ct in range(VECS // 256):
        cols = pivot_columns(ct)
        block = block - dot_hi(cols, cols, NT)
    a_ref[...] = (block + block.T) * 0.5
    invert_factor(a_ref, w_ref)
    prod_ref[...] = sum(
        dot3(vec_ref[:ROWS_DEV, ct * 256 : ct * 256 + 256], pivot_columns(ct), NT)
        for ct in range(VECS // 256)
    )
    arrived(rtgt_ref.at[pl.ds(0, DEVICES - 1)], 9)
    place_ref[...] = row_places(rtgt_ref[...].reshape(DEVICES, 128))
    place_copy = pltpu.make_async_copy(place_ref, place_smem, lsem.at[3])
    place_copy.start()
    place_copy.wait()
    arrived(recv_ref.at[pl.ds(0, 2 * (DEVICES - 1) * CAP)], 8)
    for q in range(4):
        top = q * 256

        def take(t, _, q=q):
            for u in range(32):
                line = place_smem[q * 8 + t, u] & (2 * DEVICES * CAP - 9)
                rows_ref[t * 4 + u // 8, pl.ds(u % 8, 2, 8), :] = recv_ref[pl.ds(line, 2, 8), :]
            return 0

        lax.fori_loop(0, 8, take, 0)
        rows = jnp.concatenate([rows_ref[:, h * 8 : h * 8 + 8].reshape(256, 128) for h in range(2)], axis=1)
        out_ref[top : top + 256, :] = dot3(rows - prod_ref[top : top + 256, :], w_ref[...], NT)

    for n, plane in enumerate(planes):
        left(pair_v.at[plane], 10 + n)
    left(recv_ref.at[pl.ds(0, 2 * (DEVICES - 1) * CAP)], 8)
    left(rtgt_ref.at[pl.ds(0, DEVICES - 1)], 9)

    @pl.when(core == 0)
    def _():
        left(part, 2)
        left(all0.at[others], 4)
        left(all0, 6)

    @pl.when(core == 1)
    def _():
        for n, plane in enumerate(planes):
            left(pair_i.at[plane], 14 + n)
        left(all1.at[others], 2)
        left(all1.at[others], 4)
        left(all1, 6)


VMEM_LIMIT = 52 << 20


def exchange(vectors, pivots, integrals, destination):
    vmem = pl.BlockSpec(memory_space=pltpu.VMEM)
    hbm = pl.BlockSpec(memory_space=pltpu.HBM)
    return pl.pallas_call(
        main_kernel,
        out_shape=jax.ShapeDtypeStruct((ROWS_DEV, PIVOTS), F32),
        in_specs=[pl.BlockSpec(memory_space=pltpu.SMEM), vmem, vmem, hbm, hbm],
        out_specs=vmem,
        scratch_shapes=[
            pltpu.VMEM((ROWS_DEV, PIVOTS), F32),
            pltpu.VMEM((ROWS_DEV + 8, VECS), F32),
            pltpu.VMEM((2, CHIPS, 2, 8, 128), F32),
            pltpu.VMEM((CHIPS, 8, 128), F32),
            pltpu.VMEM((CAP, DEVICES), I32),
            pltpu.SMEM((CAP, DEVICES), I32),
            pltpu.VMEM((DEVICES, 2 * CAP, 128), F32),
            pltpu.VMEM((DEVICES, 1, 128), I32),
            pltpu.VMEM((DEVICES, 1, 128), I32),
            pltpu.VMEM((CHIPS, 2, 8, 128), F32),
            pltpu.VMEM((CHIPS, 8, 128), F32),
            pltpu.VMEM((CHIPS, 3, 8, 128), F32),
            pltpu.VMEM((CHIPS - 1, 3, 8, 128), F32),
            pltpu.VMEM((3, 8, 128), F32),
            pltpu.VMEM((CHIPS, 3, 8, 128), F32),
            pltpu.VMEM((CHIPS, 2, 8, 128), F32),
            pltpu.VMEM((PIVOTS, PIVOTS), F32),
            pltpu.VMEM((PIVOTS, PIVOTS), F32),
            pltpu.VMEM((ROWS_DEV, PIVOTS), F32),
            pltpu.VMEM((2 * DEVICES * CAP, 128), F32),
            pltpu.VMEM((32, 128), I32),
            pltpu.SMEM((32, 128), I32),
            pltpu.VMEM((32, 16, 128), F32),
            pltpu.SemaphoreType.DMA((18,)),
            pltpu.SemaphoreType.DMA((18,)),
            pltpu.SemaphoreType.DMA((4,)),
        ],
        compiler_params=pltpu.CompilerParams(
            collective_id=0, has_side_effects=True, vmem_limit_bytes=VMEM_LIMIT
        ),
        name="exchange",
    )(pivots, pivots.reshape(1, -1), destination.reshape(1, -1), integrals, vectors)


def solution(mesh):
    return jax.shard_map(
        exchange,
        mesh=mesh,
        in_specs=(P(WIDE_NARROW, None), P(), P(WIDE_NARROW, None), P(WIDE_NARROW)),
        out_specs=P(WIDE_NARROW, None),
        check_vma=False,
    )
```

```python
import random

import jax, jax.numpy as jnp
from jax import lax
from jax.experimental import pallas as pl
from jax.experimental.pallas import tpu as pltpu
from jax.sharding import PartitionSpec as P

F32, BF16, I32 = jnp.float32, jnp.bfloat16, jnp.int32
HI = lax.Precision.HIGHEST
NT = (((1,), (1,)), ((), ()))
NN = (((1,), (0,)), ((), ()))
TN = (((0,), (0,)), ((), ()))
BLOCK = 64
PAIRS = 131072
ROWS_DEV = 1024
VECS = 1024
PIVOTS = 256
CAP = 16
DEVICES = PAIRS // ROWS_DEV
CHIPS = DEVICES // 2
WIDE_NARROW = ("wide", "narrow")


def dot_hi(a, b, dims=(((1,), (0,)), ((), ()))):
    return lax.dot_general(a, b, dims, precision=HI, preferred_element_type=F32)

def factor_block(s, at):
    rows = lax.broadcasted_iota(I32, (BLOCK, 2 * BLOCK), 0)
    lanes = lax.broadcasted_iota(I32, (BLOCK, 2 * BLOCK), 1)
    other = BLOCK - at
    inside = (lanes >= at) & (lanes < at + BLOCK)
    t = jnp.where(inside, s, (rows == lanes - other).astype(F32))
    done = []
    c0 = jnp.broadcast_to(t[:, at : at + 1], t.shape)
    c1 = jnp.broadcast_to(t[:, at + 1 : at + 2], t.shape)
    for j in range(0, BLOCK, 2):
        i = j % 8
        r0, r1 = t[i : i + 1, :], t[i + 1 : i + 2, :]
        a, b, c = c0[i : i + 1, :], c0[i + 1 : i + 2, :], c1[i + 1 : i + 2, :]
        inv = 1.0 / (a * c - b * b)
        p, q, s = c * inv, b * inv, a * inv
        ia = 1.0 / a
        done.append(r0 * lax.rsqrt(a))
        done.append((r1 - (b * ia) * r0) * lax.rsqrt(c - b * (b * ia)))
        if j + 2 == BLOCK:
            break
        old = t
        u0 = p * r0 - q * r1
        u1 = s * r1 - q * r0
        below = lax.broadcasted_iota(I32, t.shape, 0) > i + 1
        t = jnp.where(below, t - c0 * u0 - c1 * u1, t)
        nexts = []
        for k in (2, 3):
            x0, x1 = c0[i + k : i + k + 1, :], c1[i + k : i + k + 1, :]
            col = jnp.broadcast_to(old[:, at + j + k : at + j + k + 1], t.shape)
            nexts.append(col - c0 * (p * x0 - q * x1) - c1 * (s * x1 - q * x0))
        c0, c1 = nexts
        if (j + 2) % 8 == 0:
            t, c0, c1 = t[8:, :], c0[8:, :], c1[8:, :]
    full = jnp.concatenate(done, axis=0)
    return full[:, other : other + BLOCK]

def invert_factor(a_ref, w_ref):
    n = a_ref.shape[0]
    w_ref[...] = jnp.zeros_like(w_ref)
    for k in range(0, n, BLOCK):
        e = k + BLOCK
        base = k // 128 * 128
        inv = factor_block(a_ref[k:e, base : base + 128], k - base)
        if k == 0:
            wk = inv
        else:
            wk = jnp.concatenate([dot_hi(inv, w_ref[k:e, :k]), inv], axis=1)
        w_ref[k:e, :e] = wk
        if e < n:
            col = dot_hi(a_ref[e:, k:e], inv, NT)
            a_ref[e:, e:] = a_ref[e:, e:] - dot_hi(col, col, NT)
            w_ref[e:, :e] = w_ref[e:, :e] - dot_hi(col, wk)


def dot_bf(a, b, dims=NN):
    return lax.dot_general(a, b, dims, preferred_element_type=F32)


def bf(x):
    return x.astype(F32).astype(BF16)


def split3(x):
    hi = x.astype(BF16)
    rest = x - hi.astype(F32)
    mid = rest.astype(BF16)
    return hi, mid, (rest - mid.astype(F32)).astype(BF16)


def split2(x):
    hi = x.astype(BF16)
    return hi, (x - hi.astype(F32)).astype(BF16)


def dot3(a, b, dims):
    ah, al = split2(a)
    bh, bl = split2(b)
    return dot_bf(ah, bh, dims) + (dot_bf(ah, bl, dims) + dot_bf(al, bh, dims))


def column(row):
    return jnp.broadcast_to(row.astype(F32), (128, row.shape[1])).T.astype(I32)


def own_pivot_integrals(piv, dest, ints_ref, pint_ref):
    piv_col = column(piv)
    match = bf(
        jnp.concatenate([piv_col == dest[:, i : i + 128] for i in range(0, ROWS_DEV, 128)], axis=1)
    )
    rows = sum(dot_bf(match, part) for part in split3(ints_ref[...]))
    for ct in range(PIVOTS // 128):
        pint_ref[ct * 32 : ct * 32 + 32] = rows[:, ct * 128 : ct * 128 + 128].reshape(32, 8, 128)


def own_pivot_vectors(piv_smem, first, vec_ref, pvec_ref):
    def pick(t, _):
        for u in range(8):
            row = piv_smem[0, t * 8 + u] - first
            mine = (row >= 0) & (row < ROWS_DEV)
            values = vec_ref[pl.ds(jnp.where(mine, row, ROWS_DEV), 1), :]
            for ct in range(VECS // 128):
                pvec_ref[t // 16, ct // 2 * 16 + t % 16, ct % 2, u : u + 1, :] = values[
                    :, ct * 128 : ct * 128 + 128
                ]
        return 0

    lax.fori_loop(0, PIVOTS // 8, pick, 0)


def slot_maps(dest):
    owner = dest // ROWS_DEV
    local1 = dest - owner * ROWS_DEV + 1
    onehot = lax.broadcasted_iota(I32, (DEVICES, ROWS_DEV), 0) == owner
    onehot_bf = bf(onehot)
    before = bf(lax.broadcasted_iota(I32, (128, 128), 0) < lax.broadcasted_iota(I32, (128, 128), 1))
    ranks = []
    carry = jnp.zeros((DEVICES, 1), F32)
    for i in range(0, ROWS_DEV, 128):
        hot = onehot[:, i : i + 128]
        count = dot_bf(onehot_bf[:, i : i + 128], before) + carry
        ranks.append(jnp.sum(jnp.where(hot, count, 0.0), axis=0, keepdims=True))
        carry = carry + jnp.sum(hot.astype(F32), axis=1, keepdims=True)
    rank = jnp.concatenate(ranks, axis=1).astype(I32)
    slot = lax.broadcasted_iota(I32, (CAP, ROWS_DEV), 1)
    hit = lax.broadcasted_iota(I32, (CAP, ROWS_DEV), 0) == rank
    source = dot_bf(bf(jnp.where(hit, slot // 32, 0)), onehot_bf, NT) * 32.0
    source = source + dot_bf(bf(jnp.where(hit, slot % 32, 0)), onehot_bf, NT)
    hit = lax.broadcasted_iota(I32, (128, ROWS_DEV), 0) == rank
    target = dot_bf(onehot_bf, bf(jnp.where(hit, local1 // 32, 0)), NT) * 32.0
    target = target + dot_bf(onehot_bf, bf(jnp.where(hit, local1 % 32, 0)), NT)
    return jnp.clip(source.astype(I32), 0, ROWS_DEV - 1), target.astype(I32)


def row_places(target):
    by_slot = target.astype(F32).T.astype(I32)
    line = lax.broadcasted_iota(I32, (128, DEVICES), 0)
    block = lax.broadcasted_iota(I32, (128, DEVICES), 1)
    highs, blocks, slots = [], [], []
    for k in range(CAP):
        t = by_slot[k : k + 1, :] - 1
        highs.append(bf(line[:32] == t // 32))
        low = line == t % 32
        blocks.append(bf(jnp.where(low, block, 0)))
        slots.append(bf(jnp.where(low, k, 0)))
    high = jnp.concatenate(highs, axis=1)
    place = dot_bf(high, jnp.concatenate(blocks, axis=1), NT) * CAP
    place = place + dot_bf(high, jnp.concatenate(slots, axis=1), NT)
    place = place.astype(I32)
    return place // 8 * 16 + place % 8


def far_first(offsets):
    offsets = list(offsets)
    random.Random(7).shuffle(offsets)
    return sorted(offsets, key=lambda o: -sum(min(v, 4 - v) for v in o[:3]))


CHIP_STEPS = far_first((z, x, y) for z in range(4) for x in range(4) for y in range(4) if (z, x, y) != (0, 0, 0))
PLANE_ORDER = (2, 1, 3, 0)
ROW_SPLIT = (0, 0)
ALL_STEPS = far_first(
    (z, x, y, c)
    for z in range(4) for x in range(4) for y in range(4) for c in range(2)
    if (z, x, y, c) != (0, 0, 0, 0)
)


def main_kernel(
    index_ref, ints_hbm, vec_hbm, out_ref,
    piv_smem, ints_ref, vec_ref, pvec_ref, pint_ref, from_ref, from_smem, send_ref, tgt_ref, rtgt_ref,
    pair_v, pair_i, mine, part, tile, all0, all1, a_ref, w_ref, prod_ref,
    recv_ref, place_ref, place_smem, rows_ref, vh_ref, vl_ref, ssem, rsem, lsem,
):
    wide, narrow = lax.axis_index("wide"), lax.axis_index("narrow")
    z, core, x, y = wide // 2, wide % 2, narrow // 4, narrow % 4
    chip = z * 16 + x * 4 + y
    me = wide * 16 + narrow

    def at(dz, dx, dy, dc=0):
        oz, ox, oy, oc = (z + dz) % 4, (x + dx) % 4, (y + dy) % 4, (core + dc) % 2
        return {"wide": oz * 2 + oc, "narrow": ox * 4 + oy}, oz * 16 + ox * 4 + oy

    def send(src, dst, stage, where):
        pltpu.make_async_remote_copy(
            src_ref=src, dst_ref=dst, send_sem=ssem.at[stage], recv_sem=rsem.at[stage],
            device_id=where, device_id_type=pl.DeviceIdType.MESH,
        ).start()

    def arrived(ref, stage):
        pltpu.make_async_copy(ref, ref, rsem.at[stage]).wait()

    def left(ref, stage):
        pltpu.make_async_copy(ref, ref, ssem.at[stage]).wait()

    load_vec = pltpu.make_async_copy(vec_hbm, vec_ref.at[pl.ds(0, ROWS_DEV)], lsem.at[0])
    load_vec.start()
    load_ints = pltpu.make_async_copy(ints_hbm, ints_ref, lsem.at[1])
    load_ints.start()
    load_piv = pltpu.make_async_copy(index_ref.at[:, pl.ds(0, PIVOTS)], piv_smem, lsem.at[3])
    load_piv.start()
    barrier = pltpu.get_barrier_semaphore()
    for step in ALL_STEPS:
        pl.semaphore_signal(barrier, inc=1, device_id=at(*step)[0], device_id_type=pl.DeviceIdType.MESH)
    vec_ref[pl.ds(ROWS_DEV, 8), :] = jnp.zeros((8, VECS), F32)
    dest = index_ref[:, PIVOTS:]
    load_ints.wait()
    own_pivot_integrals(index_ref[:, :PIVOTS], dest, ints_ref, pint_ref)
    load_vec.wait()
    load_piv.wait()
    own_pivot_vectors(piv_smem, me * ROWS_DEV, vec_ref, pvec_ref)
    pl.semaphore_wait(barrier, DEVICES - 1)

    sibling = at(0, 0, 0, 1)[0]
    planes = [pl.ds(pl.multiple_of((z + dz) % 4 * 16, 16), 16) for dz in PLANE_ORDER]
    for n, plane in enumerate(planes):
        send(pvec_ref.at[1 - core, plane], pair_v.at[plane], 10 + n, sibling)

        @pl.when(core == 1)
        def _():
            send(pint_ref.at[plane], pair_i.at[plane], 14 + n, sibling)

    source, target = slot_maps(dest)
    from_ref[...] = source
    tgt_ref[...] = target.reshape(DEVICES, 1, 128)
    to_smem = pltpu.make_async_copy(from_ref, from_smem, lsem.at[2])
    to_smem.start()

    two = pl.ds(0, 2)
    step_slot = {step: i for i, step in enumerate(CHIP_STEPS)}
    for n, plane in enumerate(planes):
        arrived(pair_v.at[plane], 10 + n)
        mine[plane, 0:2] = pvec_ref[core, plane] + pair_v[plane]
        group = [step for step in CHIP_STEPS if step[0] == PLANE_ORDER[n]]

        @pl.when(core == 0)
        def _():
            arrived(pair_i.at[plane], 14 + n)
            mine[plane, 2] = pint_ref[plane] + pair_i[plane]
            for step in group:
                where, home = at(*step)
                send(mine.at[home], part.at[step_slot[step]], 2, where)

        @pl.when(core == 1)
        def _():
            for step in group:
                where, home = at(*step)
                send(mine.at[home, two], part.at[step_slot[step], two], 2, where)

    to_smem.wait()

    def pack(d, _):
        for k in range(CAP):
            row = ints_ref[pl.ds(from_smem[k, d] & (ROWS_DEV - 1), 1), :]
            send_ref[d, pl.ds(k // 8 * 16 + k % 8, 2, 8), :] = jnp.concatenate(
                [row[:, :128], row[:, 128:]], axis=0
            )
        return 0

    lax.fori_loop(0, DEVICES, pack, 0)
    steps = [at(*step)[0] for step in ALL_STEPS]

    def rows_out(begin, end):
        for i in range(begin, end):
            send(
                send_ref.at[steps[i]["wide"] * 16 + steps[i]["narrow"]],
                recv_ref.at[pl.ds(2 * i * CAP, 2 * CAP)], 8, steps[i],
            )

    rows_out(0, ROW_SPLIT[0])
    others = pl.ds(0, CHIPS - 1)

    @pl.when(core == 0)
    def _():
        arrived(part, 2)
        tile[...] = jnp.sum(part[...], axis=0) + mine[chip]
        for step in CHIP_STEPS:
            send(tile, all0.at[chip], 4, at(*step)[0])
        all0[chip] = tile[...]

    @pl.when(core == 1)
    def _():
        arrived(all1.at[others], 2)
        tile[0:2] = jnp.sum(part[:, 0:2], axis=0) + mine[chip, 0:2]
        for step in CHIP_STEPS:
            send(tile.at[two], all1.at[chip], 4, at(*step)[0])
        all1[chip] = tile[0:2]

    for i, where in enumerate(steps):
        send(tgt_ref.at[where["wide"] * 16 + where["narrow"]], rtgt_ref.at[i], 9, where)
    rtgt_ref[DEVICES - 1] = tgt_ref[me]
    rows_out(ROW_SPLIT[0], ROW_SPLIT[1])

    def halve(t, _):
        span = pl.ds(pl.multiple_of(t * 64, 64), 64)
        vh_ref[span, :], vl_ref[span, :] = split2(vec_ref[span, :])
        return 0

    lax.fori_loop(0, ROWS_DEV // 64, halve, 0)
    recv_ref[2 * (DEVICES - 1) * CAP :, :] = send_ref[me]

    @pl.when(core == 0)
    def _():
        arrived(all0.at[others], 4)
        send(all0, all0, 6, sibling)

    @pl.when(core == 1)
    def _():
        arrived(all1.at[others], 4)
        send(all1, all1, 6, sibling)

    rows_out(ROW_SPLIT[1], DEVICES - 1)

    @pl.when(core == 0)
    def _():
        arrived(all1, 6)

    @pl.when(core == 1)
    def _():
        arrived(all0, 6)

    def pivot_columns(ct):
        top, end = ct * 16, ct * 16 + 16
        return jnp.concatenate(
            [
                jnp.concatenate(
                    [all0[top:end, u].reshape(128, 128), all1[top:end, u].reshape(128, 128)], axis=0
                )
                for u in range(2)
            ],
            axis=1,
        )

    block = jnp.concatenate([all0[u * 32 : u * 32 + 32, 2].reshape(PIVOTS, 128) for u in range(2)], axis=1)
    for ct in range(VECS // 256):
        cols = pivot_columns(ct)
        block = block - dot_hi(cols, cols, NT)
    a_ref[...] = (block + block.T) * 0.5
    invert_factor(a_ref, w_ref)
    product = jnp.zeros((ROWS_DEV, PIVOTS), F32)
    for ct in range(VECS // 256):
        span = slice(ct * 256, ct * 256 + 256)
        ph, pl_ = split2(pivot_columns(ct))
        vh = vh_ref[:, span]
        product = product + (dot_bf(vh, ph, NT) + (dot_bf(vh, pl_, NT) + dot_bf(vl_ref[:, span], ph, NT)))
    prod_ref[...] = product
    arrived(rtgt_ref.at[pl.ds(0, DEVICES - 1)], 9)
    place_ref[...] = row_places(rtgt_ref[...].reshape(DEVICES, 128))
    place_copy = pltpu.make_async_copy(place_ref, place_smem, lsem.at[3])
    place_copy.start()
    place_copy.wait()
    arrived(recv_ref.at[pl.ds(0, 2 * (DEVICES - 1) * CAP)], 8)
    for q in range(4):
        top = q * 256

        def take(t, _, q=q):
            for u in range(32):
                line = place_smem[q * 8 + t, u] & (2 * DEVICES * CAP - 9)
                rows_ref[t * 4 + u // 8, pl.ds(u % 8, 2, 8), :] = recv_ref[pl.ds(line, 2, 8), :]
            return 0

        lax.fori_loop(0, 8, take, 0)
        rows = jnp.concatenate([rows_ref[:, h * 8 : h * 8 + 8].reshape(256, 128) for h in range(2)], axis=1)
        out_ref[top : top + 256, :] = dot3(rows - prod_ref[top : top + 256, :], w_ref[...], NT)

    for n, plane in enumerate(planes):
        left(pair_v.at[plane], 10 + n)
    left(recv_ref.at[pl.ds(0, 2 * (DEVICES - 1) * CAP)], 8)
    left(rtgt_ref.at[pl.ds(0, DEVICES - 1)], 9)

    @pl.when(core == 0)
    def _():
        left(part, 2)
        left(all0.at[others], 4)
        left(all0, 6)

    @pl.when(core == 1)
    def _():
        for n, plane in enumerate(planes):
            left(pair_i.at[plane], 14 + n)
        left(all1.at[others], 2)
        left(all1.at[others], 4)
        left(all1, 6)


VMEM_LIMIT = 52 << 20


def exchange(vectors, pivots, integrals, destination):
    vmem = pl.BlockSpec(memory_space=pltpu.VMEM)
    hbm = pl.BlockSpec(memory_space=pltpu.HBM)
    return pl.pallas_call(
        main_kernel,
        out_shape=jax.ShapeDtypeStruct((ROWS_DEV, PIVOTS), F32),
        in_specs=[vmem, hbm, hbm],
        out_specs=vmem,
        scratch_shapes=[
            pltpu.SMEM((1, PIVOTS), I32),
            pltpu.VMEM((ROWS_DEV, PIVOTS), F32),
            pltpu.VMEM((ROWS_DEV + 8, VECS), F32),
            pltpu.VMEM((2, CHIPS, 2, 8, 128), F32),
            pltpu.VMEM((CHIPS, 8, 128), F32),
            pltpu.VMEM((CAP, DEVICES), I32),
            pltpu.SMEM((CAP, DEVICES), I32),
            pltpu.VMEM((DEVICES, 2 * CAP, 128), F32),
            pltpu.VMEM((DEVICES, 1, 128), I32),
            pltpu.VMEM((DEVICES, 1, 128), I32),
            pltpu.VMEM((CHIPS, 2, 8, 128), F32),
            pltpu.VMEM((CHIPS, 8, 128), F32),
            pltpu.VMEM((CHIPS, 3, 8, 128), F32),
            pltpu.VMEM((CHIPS - 1, 3, 8, 128), F32),
            pltpu.VMEM((3, 8, 128), F32),
            pltpu.VMEM((CHIPS, 3, 8, 128), F32),
            pltpu.VMEM((CHIPS, 2, 8, 128), F32),
            pltpu.VMEM((PIVOTS, PIVOTS), F32),
            pltpu.VMEM((PIVOTS, PIVOTS), F32),
            pltpu.VMEM((ROWS_DEV, PIVOTS), F32),
            pltpu.VMEM((2 * DEVICES * CAP, 128), F32),
            pltpu.VMEM((32, 128), I32),
            pltpu.SMEM((32, 128), I32),
            pltpu.VMEM((32, 16, 128), F32),
            pltpu.VMEM((ROWS_DEV, VECS), BF16),
            pltpu.VMEM((ROWS_DEV, VECS), BF16),
            pltpu.SemaphoreType.DMA((18,)),
            pltpu.SemaphoreType.DMA((18,)),
            pltpu.SemaphoreType.DMA((4,)),
        ],
        compiler_params=pltpu.CompilerParams(
            collective_id=0, has_side_effects=True, vmem_limit_bytes=VMEM_LIMIT
        ),
        name="exchange",
    )(jnp.concatenate([pivots, destination]).reshape(1, -1), integrals, vectors)


def solution(mesh):
    return jax.shard_map(
        exchange,
        mesh=mesh,
        in_specs=(P(WIDE_NARROW, None), P(), P(WIDE_NARROW, None), P(WIDE_NARROW)),
        out_specs=P(WIDE_NARROW, None),
        check_vma=False,
    )
```

```python
import random

import jax, jax.numpy as jnp
from jax import lax
from jax.experimental import pallas as pl
from jax.experimental.pallas import tpu as pltpu
from jax.sharding import PartitionSpec as P

F32, BF16, I32 = jnp.float32, jnp.bfloat16, jnp.int32
HI = lax.Precision.HIGHEST
NT = (((1,), (1,)), ((), ()))
NN = (((1,), (0,)), ((), ()))
TN = (((0,), (0,)), ((), ()))
BLOCK = 64
PAIRS = 131072
ROWS_DEV = 1024
VECS = 1024
PIVOTS = 256
CAP = 16
DEVICES = PAIRS // ROWS_DEV
CHIPS = DEVICES // 2
WIDE_NARROW = ("wide", "narrow")


def dot_hi(a, b, dims=(((1,), (0,)), ((), ()))):
    return lax.dot_general(a, b, dims, precision=HI, preferred_element_type=F32)

def factor_block(s, at):
    rows = lax.broadcasted_iota(I32, (BLOCK, 2 * BLOCK), 0)
    lanes = lax.broadcasted_iota(I32, (BLOCK, 2 * BLOCK), 1)
    other = BLOCK - at
    inside = (lanes >= at) & (lanes < at + BLOCK)
    t = jnp.where(inside, s, (rows == lanes - other).astype(F32))
    done = []
    c0 = jnp.broadcast_to(t[:, at : at + 1], t.shape)
    c1 = jnp.broadcast_to(t[:, at + 1 : at + 2], t.shape)
    for j in range(0, BLOCK, 2):
        i = j % 8
        r0, r1 = t[i : i + 1, :], t[i + 1 : i + 2, :]
        a, b, c = c0[i : i + 1, :], c0[i + 1 : i + 2, :], c1[i + 1 : i + 2, :]
        inv = 1.0 / (a * c - b * b)
        p, q, s = c * inv, b * inv, a * inv
        ia = 1.0 / a
        done.append(r0 * lax.rsqrt(a))
        done.append((r1 - (b * ia) * r0) * lax.rsqrt(c - b * (b * ia)))
        if j + 2 == BLOCK:
            break
        old = t
        u0 = p * r0 - q * r1
        u1 = s * r1 - q * r0
        below = lax.broadcasted_iota(I32, t.shape, 0) > i + 1
        t = jnp.where(below, t - c0 * u0 - c1 * u1, t)
        nexts = []
        for k in (2, 3):
            x0, x1 = c0[i + k : i + k + 1, :], c1[i + k : i + k + 1, :]
            col = jnp.broadcast_to(old[:, at + j + k : at + j + k + 1], t.shape)
            nexts.append(col - c0 * (p * x0 - q * x1) - c1 * (s * x1 - q * x0))
        c0, c1 = nexts
        if (j + 2) % 8 == 0:
            t, c0, c1 = t[8:, :], c0[8:, :], c1[8:, :]
    full = jnp.concatenate(done, axis=0)
    return full[:, other : other + BLOCK]

def invert_factor(a_ref, w_ref):
    n = a_ref.shape[0]
    w_ref[...] = jnp.zeros_like(w_ref)
    for k in range(0, n, BLOCK):
        e = k + BLOCK
        base = k // 128 * 128
        inv = factor_block(a_ref[k:e, base : base + 128], k - base)
        if k == 0:
            wk = inv
        else:
            wk = jnp.concatenate([dot_hi(inv, w_ref[k:e, :k]), inv], axis=1)
        w_ref[k:e, :e] = wk
        if e < n:
            col = dot_hi(a_ref[e:, k:e], inv, NT)
            a_ref[e:, e:] = a_ref[e:, e:] - dot_hi(col, col, NT)
            w_ref[e:, :e] = w_ref[e:, :e] - dot_hi(col, wk)


def dot_bf(a, b, dims=NN):
    return lax.dot_general(a, b, dims, preferred_element_type=F32)


def bf(x):
    return x.astype(F32).astype(BF16)


def split3(x):
    hi = x.astype(BF16)
    rest = x - hi.astype(F32)
    mid = rest.astype(BF16)
    return hi, mid, (rest - mid.astype(F32)).astype(BF16)


def split2(x):
    hi = x.astype(BF16)
    return hi, (x - hi.astype(F32)).astype(BF16)


def column(row):
    return jnp.broadcast_to(row.astype(F32), (128, row.shape[1])).T.astype(I32)


def own_pivot_integrals(piv, dest, ints_ref, pint_ref):
    piv_col = column(piv)
    match = bf(
        jnp.concatenate([piv_col == dest[:, i : i + 128] for i in range(0, ROWS_DEV, 128)], axis=1)
    )
    rows = sum(dot_bf(match, part) for part in split3(ints_ref[...]))
    for ct in range(PIVOTS // 128):
        pint_ref[ct * 32 : ct * 32 + 32] = rows[:, ct * 128 : ct * 128 + 128].reshape(32, 8, 128)


def own_pivot_vectors(piv_smem, first, vec_ref, pvec_ref):
    def pick(t, _):
        for u in range(8):
            row = piv_smem[0, t * 8 + u] - first
            mine = (row >= 0) & (row < ROWS_DEV)
            values = vec_ref[pl.ds(jnp.where(mine, row, ROWS_DEV), 1), :]
            for ct in range(VECS // 128):
                pvec_ref[t // 16, ct // 2 * 16 + t % 16, ct % 2, u : u + 1, :] = values[
                    :, ct * 128 : ct * 128 + 128
                ]
        return 0

    lax.fori_loop(0, PIVOTS // 8, pick, 0)


def slot_maps(dest):
    owner = dest // ROWS_DEV
    local1 = dest - owner * ROWS_DEV + 1
    onehot = lax.broadcasted_iota(I32, (DEVICES, ROWS_DEV), 0) == owner
    onehot_bf = bf(onehot)
    before = bf(lax.broadcasted_iota(I32, (128, 128), 0) < lax.broadcasted_iota(I32, (128, 128), 1))
    ranks = []
    carry = jnp.zeros((DEVICES, 1), F32)
    for i in range(0, ROWS_DEV, 128):
        hot = onehot[:, i : i + 128]
        count = dot_bf(onehot_bf[:, i : i + 128], before) + carry
        ranks.append(jnp.sum(jnp.where(hot, count, 0.0), axis=0, keepdims=True))
        carry = carry + jnp.sum(hot.astype(F32), axis=1, keepdims=True)
    rank = jnp.concatenate(ranks, axis=1).astype(I32)
    slot = lax.broadcasted_iota(I32, (CAP, ROWS_DEV), 1)
    hit = lax.broadcasted_iota(I32, (CAP, ROWS_DEV), 0) == rank
    source = dot_bf(bf(jnp.where(hit, slot // 32, 0)), onehot_bf, NT) * 32.0
    source = source + dot_bf(bf(jnp.where(hit, slot % 32, 0)), onehot_bf, NT)
    hit = lax.broadcasted_iota(I32, (128, ROWS_DEV), 0) == rank
    target = dot_bf(onehot_bf, bf(jnp.where(hit, local1 // 32, 0)), NT) * 32.0
    target = target + dot_bf(onehot_bf, bf(jnp.where(hit, local1 % 32, 0)), NT)
    return jnp.clip(source.astype(I32), 0, ROWS_DEV - 1), target.astype(I32)


def row_places(target):
    by_slot = target.astype(F32).T.astype(I32)
    line = lax.broadcasted_iota(I32, (128, DEVICES), 0)
    block = lax.broadcasted_iota(I32, (128, DEVICES), 1)
    highs, blocks, slots = [], [], []
    for k in range(CAP):
        t = by_slot[k : k + 1, :] - 1
        highs.append(bf(line[:32] == t // 32))
        low = line == t % 32
        blocks.append(bf(jnp.where(low, block, 0)))
        slots.append(bf(jnp.where(low, k, 0)))
    high = jnp.concatenate(highs, axis=1)
    place = dot_bf(high, jnp.concatenate(blocks, axis=1), NT) * CAP
    place = place + dot_bf(high, jnp.concatenate(slots, axis=1), NT)
    place = place.astype(I32)
    return place // 8 * 16 + place % 8


def far_first(offsets):
    offsets = list(offsets)
    random.Random(7).shuffle(offsets)
    return sorted(offsets, key=lambda o: -sum(min(v, 4 - v) for v in o[:3]))


CHIP_STEPS = far_first((z, x, y) for z in range(4) for x in range(4) for y in range(4) if (z, x, y) != (0, 0, 0))
PLANE_ORDER = (2, 1, 3, 0)
ROW_SPLIT = (0, 0)
ALL_STEPS = far_first(
    (z, x, y, c)
    for z in range(4) for x in range(4) for y in range(4) for c in range(2)
    if (z, x, y, c) != (0, 0, 0, 0)
)


def main_kernel(
    index_ref, ints_hbm, vec_hbm, out_ref,
    piv_smem, ints_ref, vec_ref, pvec_ref, pint_ref, from_ref, from_smem, send_ref, tgt_ref, rtgt_ref,
    pair_v, pair_i, mine, part, tile, all0, all1, a_ref, w_ref, prod_ref,
    recv_ref, place_ref, place_smem, rows_ref, vh_ref, vl_ref, wh_ref, wl_ref, ssem, rsem, lsem,
):
    wide, narrow = lax.axis_index("wide"), lax.axis_index("narrow")
    z, core, x, y = wide // 2, wide % 2, narrow // 4, narrow % 4
    chip = z * 16 + x * 4 + y
    me = wide * 16 + narrow

    def at(dz, dx, dy, dc=0):
        oz, ox, oy, oc = (z + dz) % 4, (x + dx) % 4, (y + dy) % 4, (core + dc) % 2
        return {"wide": oz * 2 + oc, "narrow": ox * 4 + oy}, oz * 16 + ox * 4 + oy

    def send(src, dst, stage, where):
        pltpu.make_async_remote_copy(
            src_ref=src, dst_ref=dst, send_sem=ssem.at[stage], recv_sem=rsem.at[stage],
            device_id=where, device_id_type=pl.DeviceIdType.MESH,
        ).start()

    def arrived(ref, stage):
        pltpu.make_async_copy(ref, ref, rsem.at[stage]).wait()

    def left(ref, stage):
        pltpu.make_async_copy(ref, ref, ssem.at[stage]).wait()

    load_vec = pltpu.make_async_copy(vec_hbm, vec_ref.at[pl.ds(0, ROWS_DEV)], lsem.at[0])
    load_vec.start()
    load_ints = pltpu.make_async_copy(ints_hbm, ints_ref, lsem.at[1])
    load_ints.start()
    load_piv = pltpu.make_async_copy(index_ref.at[:, pl.ds(0, PIVOTS)], piv_smem, lsem.at[3])
    load_piv.start()
    barrier = pltpu.get_barrier_semaphore()
    for step in ALL_STEPS:
        pl.semaphore_signal(barrier, inc=1, device_id=at(*step)[0], device_id_type=pl.DeviceIdType.MESH)
    vec_ref[pl.ds(ROWS_DEV, 8), :] = jnp.zeros((8, VECS), F32)
    dest = index_ref[:, PIVOTS:]
    load_ints.wait()
    own_pivot_integrals(index_ref[:, :PIVOTS], dest, ints_ref, pint_ref)
    load_vec.wait()
    load_piv.wait()
    own_pivot_vectors(piv_smem, me * ROWS_DEV, vec_ref, pvec_ref)
    pl.semaphore_wait(barrier, DEVICES - 1)

    sibling = at(0, 0, 0, 1)[0]
    planes = [pl.ds(pl.multiple_of((z + dz) % 4 * 16, 16), 16) for dz in PLANE_ORDER]
    for n, plane in enumerate(planes):
        send(pvec_ref.at[1 - core, plane], pair_v.at[plane], 10 + n, sibling)

        @pl.when(core == 1)
        def _():
            send(pint_ref.at[plane], pair_i.at[plane], 14 + n, sibling)

    source, target = slot_maps(dest)
    from_ref[...] = source
    tgt_ref[...] = target.reshape(DEVICES, 1, 128)
    to_smem = pltpu.make_async_copy(from_ref, from_smem, lsem.at[2])
    to_smem.start()

    two = pl.ds(0, 2)
    step_slot = {step: i for i, step in enumerate(CHIP_STEPS)}
    for n, plane in enumerate(planes):
        arrived(pair_v.at[plane], 10 + n)
        mine[plane, 0:2] = pvec_ref[core, plane] + pair_v[plane]
        group = [step for step in CHIP_STEPS if step[0] == PLANE_ORDER[n]]

        @pl.when(core == 0)
        def _():
            arrived(pair_i.at[plane], 14 + n)
            mine[plane, 2] = pint_ref[plane] + pair_i[plane]
            for step in group:
                where, home = at(*step)
                send(mine.at[home], part.at[step_slot[step]], 2, where)

        @pl.when(core == 1)
        def _():
            for step in group:
                where, home = at(*step)
                send(mine.at[home, two], part.at[step_slot[step], two], 2, where)

    to_smem.wait()

    def pack(d, _):
        for k in range(CAP):
            row = ints_ref[pl.ds(from_smem[k, d] & (ROWS_DEV - 1), 1), :]
            send_ref[d, pl.ds(k // 8 * 16 + k % 8, 2, 8), :] = jnp.concatenate(
                [row[:, :128], row[:, 128:]], axis=0
            )
        return 0

    lax.fori_loop(0, DEVICES, pack, 0)
    steps = [at(*step)[0] for step in ALL_STEPS]

    def rows_out(begin, end):
        for i in range(begin, end):
            send(
                send_ref.at[steps[i]["wide"] * 16 + steps[i]["narrow"]],
                recv_ref.at[pl.ds(2 * i * CAP, 2 * CAP)], 8, steps[i],
            )

    rows_out(0, ROW_SPLIT[0])
    others = pl.ds(0, CHIPS - 1)

    @pl.when(core == 0)
    def _():
        arrived(part, 2)
        tile[...] = jnp.sum(part[...], axis=0) + mine[chip]
        for step in CHIP_STEPS:
            send(tile, all0.at[chip], 4, at(*step)[0])
        all0[chip] = tile[...]

    @pl.when(core == 1)
    def _():
        arrived(all1.at[others], 2)
        tile[0:2] = jnp.sum(part[:, 0:2], axis=0) + mine[chip, 0:2]
        for step in CHIP_STEPS:
            send(tile.at[two], all1.at[chip], 4, at(*step)[0])
        all1[chip] = tile[0:2]

    for i, where in enumerate(steps):
        send(tgt_ref.at[where["wide"] * 16 + where["narrow"]], rtgt_ref.at[i], 9, where)
    rtgt_ref[DEVICES - 1] = tgt_ref[me]
    rows_out(ROW_SPLIT[0], ROW_SPLIT[1])

    def halve(t, _):
        span = pl.ds(pl.multiple_of(t * 64, 64), 64)
        vh_ref[span, :], vl_ref[span, :] = split2(vec_ref[span, :])
        return 0

    lax.fori_loop(0, ROWS_DEV // 64, halve, 0)
    recv_ref[2 * (DEVICES - 1) * CAP :, :] = send_ref[me]

    @pl.when(core == 0)
    def _():
        arrived(all0.at[others], 4)
        send(all0, all0, 6, sibling)

    @pl.when(core == 1)
    def _():
        arrived(all1.at[others], 4)
        send(all1, all1, 6, sibling)

    rows_out(ROW_SPLIT[1], DEVICES - 1)

    @pl.when(core == 0)
    def _():
        arrived(all1, 6)

    @pl.when(core == 1)
    def _():
        arrived(all0, 6)

    def pivot_columns(ct):
        top, end = ct * 16, ct * 16 + 16
        return jnp.concatenate(
            [
                jnp.concatenate(
                    [all0[top:end, u].reshape(128, 128), all1[top:end, u].reshape(128, 128)], axis=0
                )
                for u in range(2)
            ],
            axis=1,
        )

    block = jnp.concatenate([all0[u * 32 : u * 32 + 32, 2].reshape(PIVOTS, 128) for u in range(2)], axis=1)
    for ct in range(VECS // 256):
        cols = pivot_columns(ct)
        block = block - dot_hi(cols, cols, NT)
    a_ref[...] = (block + block.T) * 0.5
    invert_factor(a_ref, w_ref)
    wh_ref[...], wl_ref[...] = split2(w_ref[...])
    product = jnp.zeros((ROWS_DEV, PIVOTS), F32)
    for ct in range(VECS // 256):
        span = slice(ct * 256, ct * 256 + 256)
        ph, pl_ = split2(pivot_columns(ct))
        vh = vh_ref[:, span]
        product = product + (dot_bf(vh, ph, NT) + (dot_bf(vh, pl_, NT) + dot_bf(vl_ref[:, span], ph, NT)))
    prod_ref[...] = product
    arrived(rtgt_ref.at[pl.ds(0, DEVICES - 1)], 9)
    place_ref[...] = row_places(rtgt_ref[...].reshape(DEVICES, 128))
    place_copy = pltpu.make_async_copy(place_ref, place_smem, lsem.at[3])
    place_copy.start()
    place_copy.wait()
    arrived(recv_ref.at[pl.ds(0, 2 * (DEVICES - 1) * CAP)], 8)

    def take(q):
        for t in range(CHUNK // 32):
            for u in range(32):
                line = place_smem[q * (CHUNK // 32) + t, u] & (2 * DEVICES * CAP - 9)
                rows_ref[t * 4 + u // 8, pl.ds(u % 8, 2, 8), :] = recv_ref[pl.ds(line, 2, 8), :]

    def finish(q, rows):
        span = pl.ds(pl.multiple_of(q * CHUNK, CHUNK), CHUNK)
        rh, rl = split2(rows - prod_ref[span, :])
        wh = wh_ref[...]
        out_ref[span, :] = dot_bf(rh, wh, NT) + (dot_bf(rh, wl_ref[...], NT) + dot_bf(rl, wh, NT))

    def gathered():
        return jnp.concatenate([rows_ref[:, h * 8 : h * 8 + 8].reshape(CHUNK, 128) for h in range(2)], axis=1)

    def step(q, _):
        rows = gathered()
        take(q + 1)
        finish(q, rows)
        return 0

    take(0)
    lax.fori_loop(0, ROWS_DEV // CHUNK - 1, step, 0)
    finish(ROWS_DEV // CHUNK - 1, gathered())

    for n, plane in enumerate(planes):
        left(pair_v.at[plane], 10 + n)
    left(recv_ref.at[pl.ds(0, 2 * (DEVICES - 1) * CAP)], 8)
    left(rtgt_ref.at[pl.ds(0, DEVICES - 1)], 9)

    @pl.when(core == 0)
    def _():
        left(part, 2)
        left(all0.at[others], 4)
        left(all0, 6)

    @pl.when(core == 1)
    def _():
        for n, plane in enumerate(planes):
            left(pair_i.at[plane], 14 + n)
        left(all1.at[others], 2)
        left(all1.at[others], 4)
        left(all1, 6)


VMEM_LIMIT = 52 << 20
CHUNK = 128


def exchange(vectors, pivots, integrals, destination):
    vmem = pl.BlockSpec(memory_space=pltpu.VMEM)
    hbm = pl.BlockSpec(memory_space=pltpu.HBM)
    return pl.pallas_call(
        main_kernel,
        out_shape=jax.ShapeDtypeStruct((ROWS_DEV, PIVOTS), F32),
        in_specs=[vmem, hbm, hbm],
        out_specs=vmem,
        scratch_shapes=[
            pltpu.SMEM((1, PIVOTS), I32),
            pltpu.VMEM((ROWS_DEV, PIVOTS), F32),
            pltpu.VMEM((ROWS_DEV + 8, VECS), F32),
            pltpu.VMEM((2, CHIPS, 2, 8, 128), F32),
            pltpu.VMEM((CHIPS, 8, 128), F32),
            pltpu.VMEM((CAP, DEVICES), I32),
            pltpu.SMEM((CAP, DEVICES), I32),
            pltpu.VMEM((DEVICES, 2 * CAP, 128), F32),
            pltpu.VMEM((DEVICES, 1, 128), I32),
            pltpu.VMEM((DEVICES, 1, 128), I32),
            pltpu.VMEM((CHIPS, 2, 8, 128), F32),
            pltpu.VMEM((CHIPS, 8, 128), F32),
            pltpu.VMEM((CHIPS, 3, 8, 128), F32),
            pltpu.VMEM((CHIPS - 1, 3, 8, 128), F32),
            pltpu.VMEM((3, 8, 128), F32),
            pltpu.VMEM((CHIPS, 3, 8, 128), F32),
            pltpu.VMEM((CHIPS, 2, 8, 128), F32),
            pltpu.VMEM((PIVOTS, PIVOTS), F32),
            pltpu.VMEM((PIVOTS, PIVOTS), F32),
            pltpu.VMEM((ROWS_DEV, PIVOTS), F32),
            pltpu.VMEM((2 * DEVICES * CAP, 128), F32),
            pltpu.VMEM((32, 128), I32),
            pltpu.SMEM((32, 128), I32),
            pltpu.VMEM((CHUNK // 8, 16, 128), F32),
            pltpu.VMEM((ROWS_DEV, VECS), BF16),
            pltpu.VMEM((ROWS_DEV, VECS), BF16),
            pltpu.VMEM((PIVOTS, PIVOTS), BF16),
            pltpu.VMEM((PIVOTS, PIVOTS), BF16),
            pltpu.SemaphoreType.DMA((18,)),
            pltpu.SemaphoreType.DMA((18,)),
            pltpu.SemaphoreType.DMA((4,)),
        ],
        compiler_params=pltpu.CompilerParams(
            collective_id=0, has_side_effects=True, vmem_limit_bytes=VMEM_LIMIT
        ),
        name="exchange",
    )(jnp.concatenate([pivots, destination]).reshape(1, -1), integrals, vectors)


def solution(mesh):
    return jax.shard_map(
        exchange,
        mesh=mesh,
        in_specs=(P(WIDE_NARROW, None), P(), P(WIDE_NARROW, None), P(WIDE_NARROW)),
        out_specs=P(WIDE_NARROW, None),
        check_vma=False,
    )
```

```python
import random

import jax, jax.numpy as jnp
from jax import lax
from jax.experimental import pallas as pl
from jax.experimental.pallas import tpu as pltpu
from jax.sharding import PartitionSpec as P

F32, BF16, I32 = jnp.float32, jnp.bfloat16, jnp.int32
HI = lax.Precision.HIGHEST
NT = (((1,), (1,)), ((), ()))
NN = (((1,), (0,)), ((), ()))
TN = (((0,), (0,)), ((), ()))
BLOCK = 64
PAIRS = 131072
ROWS_DEV = 1024
VECS = 1024
PIVOTS = 256
CAP = 16
DEVICES = PAIRS // ROWS_DEV
CHIPS = DEVICES // 2
WIDE_NARROW = ("wide", "narrow")


def dot_hi(a, b, dims=(((1,), (0,)), ((), ()))):
    return lax.dot_general(a, b, dims, precision=HI, preferred_element_type=F32)

def factor_block(s, at):
    rows = lax.broadcasted_iota(I32, (BLOCK, 2 * BLOCK), 0)
    lanes = lax.broadcasted_iota(I32, (BLOCK, 2 * BLOCK), 1)
    other = BLOCK - at
    inside = (lanes >= at) & (lanes < at + BLOCK)
    t = jnp.where(inside, s, (rows == lanes - other).astype(F32))
    done = []
    c0 = jnp.broadcast_to(t[:, at : at + 1], t.shape)
    c1 = jnp.broadcast_to(t[:, at + 1 : at + 2], t.shape)
    for j in range(0, BLOCK, 2):
        i = j % 8
        r0, r1 = t[i : i + 1, :], t[i + 1 : i + 2, :]
        a, b, c = c0[i : i + 1, :], c0[i + 1 : i + 2, :], c1[i + 1 : i + 2, :]
        inv = 1.0 / (a * c - b * b)
        p, q, s = c * inv, b * inv, a * inv
        ia = 1.0 / a
        done.append(r0 * lax.rsqrt(a))
        done.append((r1 - (b * ia) * r0) * lax.rsqrt(c - b * (b * ia)))
        if j + 2 == BLOCK:
            break
        old = t
        u0 = p * r0 - q * r1
        u1 = s * r1 - q * r0
        below = lax.broadcasted_iota(I32, t.shape, 0) > i + 1
        t = jnp.where(below, t - c0 * u0 - c1 * u1, t)
        nexts = []
        for k in (2, 3):
            x0, x1 = c0[i + k : i + k + 1, :], c1[i + k : i + k + 1, :]
            col = jnp.broadcast_to(old[:, at + j + k : at + j + k + 1], t.shape)
            nexts.append(col - c0 * (p * x0 - q * x1) - c1 * (s * x1 - q * x0))
        c0, c1 = nexts
        if (j + 2) % 8 == 0:
            t, c0, c1 = t[8:, :], c0[8:, :], c1[8:, :]
    full = jnp.concatenate(done, axis=0)
    return full[:, other : other + BLOCK]

def invert_factor(a_ref, w_ref):
    n = a_ref.shape[0]
    w_ref[...] = jnp.zeros_like(w_ref)
    for k in range(0, n, BLOCK):
        e = k + BLOCK
        base = k // 128 * 128
        inv = factor_block(a_ref[k:e, base : base + 128], k - base)
        if k == 0:
            wk = inv
        else:
            wk = jnp.concatenate([dot_hi(inv, w_ref[k:e, :k]), inv], axis=1)
        w_ref[k:e, :e] = wk
        if e < n:
            col = dot_hi(a_ref[e:, k:e], inv, NT)
            a_ref[e:, e:] = a_ref[e:, e:] - dot_hi(col, col, NT)
            w_ref[e:, :e] = w_ref[e:, :e] - dot_hi(col, wk)


def dot_bf(a, b, dims=NN):
    return lax.dot_general(a, b, dims, preferred_element_type=F32)


def bf(x):
    return x.astype(F32).astype(BF16)


def split3(x):
    hi = x.astype(BF16)
    rest = x - hi.astype(F32)
    mid = rest.astype(BF16)
    return hi, mid, (rest - mid.astype(F32)).astype(BF16)


def split2(x):
    hi = x.astype(BF16)
    return hi, (x - hi.astype(F32)).astype(BF16)


def column(row):
    return jnp.broadcast_to(row.astype(F32), (128, row.shape[1])).T.astype(I32)


def own_pivot_integrals(piv, dest, ints_ref, pint_ref):
    piv_col = column(piv)
    match = bf(
        jnp.concatenate([piv_col == dest[:, i : i + 128] for i in range(0, ROWS_DEV, 128)], axis=1)
    )
    rows = sum(dot_bf(match, part) for part in split3(ints_ref[...]))
    for ct in range(PIVOTS // 128):
        pint_ref[ct * 32 : ct * 32 + 32] = rows[:, ct * 128 : ct * 128 + 128].reshape(32, 8, 128)


def own_pivot_vectors(piv_smem, first, vec_ref, pvec_ref):
    def pick(t, _):
        for u in range(8):
            row = piv_smem[0, t * 8 + u] - first
            mine = (row >= 0) & (row < ROWS_DEV)
            values = vec_ref[pl.ds(jnp.where(mine, row, ROWS_DEV), 1), :]
            for ct in range(VECS // 128):
                pvec_ref[t // 16, ct // 2 * 16 + t % 16, ct % 2, u : u + 1, :] = values[
                    :, ct * 128 : ct * 128 + 128
                ]
        return 0

    lax.fori_loop(0, PIVOTS // 8, pick, 0)


def slot_maps(dest):
    owner = dest // ROWS_DEV
    local1 = dest - owner * ROWS_DEV + 1
    onehot = lax.broadcasted_iota(I32, (DEVICES, ROWS_DEV), 0) == owner
    onehot_bf = bf(onehot)
    before = bf(lax.broadcasted_iota(I32, (128, 128), 0) < lax.broadcasted_iota(I32, (128, 128), 1))
    ranks = []
    carry = jnp.zeros((DEVICES, 1), F32)
    for i in range(0, ROWS_DEV, 128):
        hot = onehot[:, i : i + 128]
        count = dot_bf(onehot_bf[:, i : i + 128], before) + carry
        ranks.append(jnp.sum(jnp.where(hot, count, 0.0), axis=0, keepdims=True))
        carry = carry + jnp.sum(hot.astype(F32), axis=1, keepdims=True)
    rank = jnp.concatenate(ranks, axis=1).astype(I32)
    slot = lax.broadcasted_iota(I32, (CAP, ROWS_DEV), 1)
    hit = lax.broadcasted_iota(I32, (CAP, ROWS_DEV), 0) == rank
    source = dot_bf(bf(jnp.where(hit, slot // 32, 0)), onehot_bf, NT) * 32.0
    source = source + dot_bf(bf(jnp.where(hit, slot % 32, 0)), onehot_bf, NT)
    hit = lax.broadcasted_iota(I32, (128, ROWS_DEV), 0) == rank
    target = dot_bf(onehot_bf, bf(jnp.where(hit, local1 // 32, 0)), NT) * 32.0
    target = target + dot_bf(onehot_bf, bf(jnp.where(hit, local1 % 32, 0)), NT)
    return jnp.clip(source.astype(I32), 0, ROWS_DEV - 1), target.astype(I32)


def row_places(target):
    by_slot = target.astype(F32).T.astype(I32)
    line = lax.broadcasted_iota(I32, (128, DEVICES), 0)
    block = lax.broadcasted_iota(I32, (128, DEVICES), 1)
    highs, blocks, slots = [], [], []
    for k in range(CAP):
        t = by_slot[k : k + 1, :] - 1
        highs.append(bf(line[:32] == t // 32))
        low = line == t % 32
        blocks.append(bf(jnp.where(low, block, 0)))
        slots.append(bf(jnp.where(low, k, 0)))
    high = jnp.concatenate(highs, axis=1)
    place = dot_bf(high, jnp.concatenate(blocks, axis=1), NT) * CAP
    place = place + dot_bf(high, jnp.concatenate(slots, axis=1), NT)
    place = place.astype(I32)
    return place // 8 * 16 + place % 8


def far_first(offsets):
    offsets = list(offsets)
    random.Random(3).shuffle(offsets)
    return sorted(offsets, key=lambda o: -sum(min(v, 4 - v) for v in o[:3]))


CHIP_STEPS = far_first((z, x, y) for z in range(4) for x in range(4) for y in range(4) if (z, x, y) != (0, 0, 0))
PLANE_ORDER = (2, 1, 3, 0)
ROW_SPLIT = (0, 0)
ALL_STEPS = far_first(
    (z, x, y, c)
    for z in range(4) for x in range(4) for y in range(4) for c in range(2)
    if (z, x, y, c) != (0, 0, 0, 0)
)


def main_kernel(
    index_ref, ints_hbm, vec_hbm, out_ref,
    piv_smem, ints_ref, vec_ref, pvec_ref, pint_ref, from_ref, from_smem, send_ref, tgt_ref, rtgt_ref,
    pair_v, pair_i, mine, part, tile, all0, all1, a_ref, w_ref, prod_ref,
    recv_ref, place_ref, place_smem, rows_ref, vh_ref, vl_ref, wh_ref, wl_ref, ssem, rsem, lsem,
):
    wide, narrow = lax.axis_index("wide"), lax.axis_index("narrow")
    z, core, x, y = wide // 2, wide % 2, narrow // 4, narrow % 4
    chip = z * 16 + x * 4 + y
    me = wide * 16 + narrow

    def at(dz, dx, dy, dc=0):
        oz, ox, oy, oc = (z + dz) % 4, (x + dx) % 4, (y + dy) % 4, (core + dc) % 2
        return {"wide": oz * 2 + oc, "narrow": ox * 4 + oy}, oz * 16 + ox * 4 + oy

    def send(src, dst, stage, where):
        pltpu.make_async_remote_copy(
            src_ref=src, dst_ref=dst, send_sem=ssem.at[stage], recv_sem=rsem.at[stage],
            device_id=where, device_id_type=pl.DeviceIdType.MESH,
        ).start()

    def arrived(ref, stage):
        pltpu.make_async_copy(ref, ref, rsem.at[stage]).wait()

    def left(ref, stage):
        pltpu.make_async_copy(ref, ref, ssem.at[stage]).wait()

    load_vec = pltpu.make_async_copy(vec_hbm, vec_ref.at[pl.ds(0, ROWS_DEV)], lsem.at[0])
    load_vec.start()
    load_ints = pltpu.make_async_copy(ints_hbm, ints_ref, lsem.at[1])
    load_ints.start()
    load_piv = pltpu.make_async_copy(index_ref.at[:, pl.ds(0, PIVOTS)], piv_smem, lsem.at[3])
    load_piv.start()
    barrier = pltpu.get_barrier_semaphore()
    for step in ALL_STEPS:
        pl.semaphore_signal(barrier, inc=1, device_id=at(*step)[0], device_id_type=pl.DeviceIdType.MESH)
    vec_ref[pl.ds(ROWS_DEV, 8), :] = jnp.zeros((8, VECS), F32)
    dest = index_ref[:, PIVOTS:]
    load_ints.wait()
    own_pivot_integrals(index_ref[:, :PIVOTS], dest, ints_ref, pint_ref)
    load_vec.wait()
    load_piv.wait()
    own_pivot_vectors(piv_smem, me * ROWS_DEV, vec_ref, pvec_ref)
    pl.semaphore_wait(barrier, DEVICES - 1)

    sibling = at(0, 0, 0, 1)[0]
    planes = [pl.ds(pl.multiple_of((z + dz) % 4 * 16, 16), 16) for dz in PLANE_ORDER]
    for n, plane in enumerate(planes):
        send(pvec_ref.at[1 - core, plane], pair_v.at[plane], 10 + n, sibling)

        @pl.when(core == 1)
        def _():
            send(pint_ref.at[plane], pair_i.at[plane], 14 + n, sibling)

    source, target = slot_maps(dest)
    from_ref[...] = source
    tgt_ref[...] = target.reshape(DEVICES, 1, 128)
    to_smem = pltpu.make_async_copy(from_ref, from_smem, lsem.at[2])
    to_smem.start()

    two = pl.ds(0, 2)
    step_slot = {step: i for i, step in enumerate(CHIP_STEPS)}
    for n, plane in enumerate(planes):
        arrived(pair_v.at[plane], 10 + n)
        mine[plane, 0:2] = pvec_ref[core, plane] + pair_v[plane]
        group = [step for step in CHIP_STEPS if step[0] == PLANE_ORDER[n]]

        @pl.when(core == 0)
        def _():
            arrived(pair_i.at[plane], 14 + n)
            mine[plane, 2] = pint_ref[plane] + pair_i[plane]
            for step in group:
                where, home = at(*step)
                send(mine.at[home], part.at[step_slot[step]], 2, where)

        @pl.when(core == 1)
        def _():
            for step in group:
                where, home = at(*step)
                send(mine.at[home, two], part.at[step_slot[step], two], 2, where)

    to_smem.wait()

    def pack(d, _):
        for k in range(CAP):
            row = ints_ref[pl.ds(from_smem[k, d] & (ROWS_DEV - 1), 1), :]
            send_ref[d, pl.ds(k // 8 * 16 + k % 8, 2, 8), :] = jnp.concatenate(
                [row[:, :128], row[:, 128:]], axis=0
            )
        return 0

    lax.fori_loop(0, DEVICES, pack, 0)
    steps = [at(*step)[0] for step in ALL_STEPS]

    def rows_out(begin, end):
        for i in range(begin, end):
            send(
                send_ref.at[steps[i]["wide"] * 16 + steps[i]["narrow"]],
                recv_ref.at[pl.ds(2 * i * CAP, 2 * CAP)], 8, steps[i],
            )

    rows_out(0, ROW_SPLIT[0])
    others = pl.ds(0, CHIPS - 1)

    @pl.when(core == 0)
    def _():
        arrived(part, 2)
        tile[...] = jnp.sum(part[...], axis=0) + mine[chip]
        for step in CHIP_STEPS:
            send(tile, all0.at[chip], 4, at(*step)[0])
        all0[chip] = tile[...]

    @pl.when(core == 1)
    def _():
        arrived(all1.at[others], 2)
        tile[0:2] = jnp.sum(part[:, 0:2], axis=0) + mine[chip, 0:2]
        for step in CHIP_STEPS:
            send(tile.at[two], all1.at[chip], 4, at(*step)[0])
        all1[chip] = tile[0:2]

    for i, where in enumerate(steps):
        send(tgt_ref.at[where["wide"] * 16 + where["narrow"]], rtgt_ref.at[i], 9, where)
    rtgt_ref[DEVICES - 1] = tgt_ref[me]
    rows_out(ROW_SPLIT[0], ROW_SPLIT[1])

    def halve(t, _):
        span = pl.ds(pl.multiple_of(t * 64, 64), 64)
        vh_ref[span, :], vl_ref[span, :] = split2(vec_ref[span, :])
        return 0

    lax.fori_loop(0, ROWS_DEV // 64, halve, 0)
    recv_ref[2 * (DEVICES - 1) * CAP :, :] = send_ref[me]

    @pl.when(core == 0)
    def _():
        arrived(all0.at[others], 4)
        send(all0, all0, 6, sibling)

    @pl.when(core == 1)
    def _():
        arrived(all1.at[others], 4)
        send(all1, all1, 6, sibling)

    rows_out(ROW_SPLIT[1], DEVICES - 1)

    @pl.when(core == 0)
    def _():
        arrived(all1, 6)

    @pl.when(core == 1)
    def _():
        arrived(all0, 6)

    def pivot_columns(ct):
        top, end = ct * 16, ct * 16 + 16
        return jnp.concatenate(
            [
                jnp.concatenate(
                    [all0[top:end, u].reshape(128, 128), all1[top:end, u].reshape(128, 128)], axis=0
                )
                for u in range(2)
            ],
            axis=1,
        )

    block = jnp.concatenate([all0[u * 32 : u * 32 + 32, 2].reshape(PIVOTS, 128) for u in range(2)], axis=1)
    for ct in range(VECS // 256):
        cols = pivot_columns(ct)
        block = block - dot_hi(cols, cols, NT)
    a_ref[...] = (block + block.T) * 0.5
    invert_factor(a_ref, w_ref)
    wh_ref[...], wl_ref[...] = split2(w_ref[...])
    product = jnp.zeros((ROWS_DEV, PIVOTS), F32)
    for ct in range(VECS // 256):
        span = slice(ct * 256, ct * 256 + 256)
        ph, pl_ = split2(pivot_columns(ct))
        vh = vh_ref[:, span]
        product = product + (dot_bf(vh, ph, NT) + (dot_bf(vh, pl_, NT) + dot_bf(vl_ref[:, span], ph, NT)))
    prod_ref[...] = product
    arrived(rtgt_ref.at[pl.ds(0, DEVICES - 1)], 9)
    place_ref[...] = row_places(rtgt_ref[...].reshape(DEVICES, 128))
    place_copy = pltpu.make_async_copy(place_ref, place_smem, lsem.at[3])
    place_copy.start()
    place_copy.wait()
    arrived(recv_ref.at[pl.ds(0, 2 * (DEVICES - 1) * CAP)], 8)

    def take(q):
        for t in range(CHUNK // 32):
            for u in range(32):
                line = place_smem[q * (CHUNK // 32) + t, u] & (2 * DEVICES * CAP - 9)
                rows_ref[t * 4 + u // 8, pl.ds(u % 8, 2, 8), :] = recv_ref[pl.ds(line, 2, 8), :]

    def finish(q, rows):
        span = pl.ds(pl.multiple_of(q * CHUNK, CHUNK), CHUNK)
        rh, rl = split2(rows - prod_ref[span, :])
        wh = wh_ref[...]
        out_ref[span, :] = dot_bf(rh, wh, NT) + (dot_bf(rh, wl_ref[...], NT) + dot_bf(rl, wh, NT))

    def gathered():
        return jnp.concatenate([rows_ref[:, h * 8 : h * 8 + 8].reshape(CHUNK, 128) for h in range(2)], axis=1)

    def step(q, _):
        rows = gathered()
        take(q + 1)
        finish(q, rows)
        return 0

    take(0)
    lax.fori_loop(0, ROWS_DEV // CHUNK - 1, step, 0)
    finish(ROWS_DEV // CHUNK - 1, gathered())

    for n, plane in enumerate(planes):
        left(pair_v.at[plane], 10 + n)
    left(recv_ref.at[pl.ds(0, 2 * (DEVICES - 1) * CAP)], 8)
    left(rtgt_ref.at[pl.ds(0, DEVICES - 1)], 9)

    @pl.when(core == 0)
    def _():
        left(part, 2)
        left(all0.at[others], 4)
        left(all0, 6)

    @pl.when(core == 1)
    def _():
        for n, plane in enumerate(planes):
            left(pair_i.at[plane], 14 + n)
        left(all1.at[others], 2)
        left(all1.at[others], 4)
        left(all1, 6)


VMEM_LIMIT = 52 << 20
CHUNK = 256


def exchange(vectors, pivots, integrals, destination):
    vmem = pl.BlockSpec(memory_space=pltpu.VMEM)
    hbm = pl.BlockSpec(memory_space=pltpu.HBM)
    return pl.pallas_call(
        main_kernel,
        out_shape=jax.ShapeDtypeStruct((ROWS_DEV, PIVOTS), F32),
        in_specs=[vmem, hbm, hbm],
        out_specs=vmem,
        scratch_shapes=[
            pltpu.SMEM((1, PIVOTS), I32),
            pltpu.VMEM((ROWS_DEV, PIVOTS), F32),
            pltpu.VMEM((ROWS_DEV + 8, VECS), F32),
            pltpu.VMEM((2, CHIPS, 2, 8, 128), F32),
            pltpu.VMEM((CHIPS, 8, 128), F32),
            pltpu.VMEM((CAP, DEVICES), I32),
            pltpu.SMEM((CAP, DEVICES), I32),
            pltpu.VMEM((DEVICES, 2 * CAP, 128), F32),
            pltpu.VMEM((DEVICES, 1, 128), I32),
            pltpu.VMEM((DEVICES, 1, 128), I32),
            pltpu.VMEM((CHIPS, 2, 8, 128), F32),
            pltpu.VMEM((CHIPS, 8, 128), F32),
            pltpu.VMEM((CHIPS, 3, 8, 128), F32),
            pltpu.VMEM((CHIPS - 1, 3, 8, 128), F32),
            pltpu.VMEM((3, 8, 128), F32),
            pltpu.VMEM((CHIPS, 3, 8, 128), F32),
            pltpu.VMEM((CHIPS, 2, 8, 128), F32),
            pltpu.VMEM((PIVOTS, PIVOTS), F32),
            pltpu.VMEM((PIVOTS, PIVOTS), F32),
            pltpu.VMEM((ROWS_DEV, PIVOTS), F32),
            pltpu.VMEM((2 * DEVICES * CAP, 128), F32),
            pltpu.VMEM((32, 128), I32),
            pltpu.SMEM((32, 128), I32),
            pltpu.VMEM((CHUNK // 8, 16, 128), F32),
            pltpu.VMEM((ROWS_DEV, VECS), BF16),
            pltpu.VMEM((ROWS_DEV, VECS), BF16),
            pltpu.VMEM((PIVOTS, PIVOTS), BF16),
            pltpu.VMEM((PIVOTS, PIVOTS), BF16),
            pltpu.SemaphoreType.DMA((18,)),
            pltpu.SemaphoreType.DMA((18,)),
            pltpu.SemaphoreType.DMA((4,)),
        ],
        compiler_params=pltpu.CompilerParams(
            collective_id=0, has_side_effects=True, vmem_limit_bytes=VMEM_LIMIT
        ),
        name="exchange",
    )(jnp.concatenate([pivots, destination]).reshape(1, -1), integrals, vectors)


def solution(mesh):
    return jax.shard_map(
        exchange,
        mesh=mesh,
        in_specs=(P(WIDE_NARROW, None), P(), P(WIDE_NARROW, None), P(WIDE_NARROW)),
        out_specs=P(WIDE_NARROW, None),
        check_vma=False,
    )
```

```python
import random

import jax, jax.numpy as jnp
from jax import lax
from jax.experimental import pallas as pl
from jax.experimental.pallas import tpu as pltpu
from jax.sharding import PartitionSpec as P

F32, BF16, I32 = jnp.float32, jnp.bfloat16, jnp.int32
HI = lax.Precision.HIGHEST
NT = (((1,), (1,)), ((), ()))
NN = (((1,), (0,)), ((), ()))
TN = (((0,), (0,)), ((), ()))
BLOCK = 64
PAIRS = 131072
ROWS_DEV = 1024
VECS = 1024
PIVOTS = 256
CAP = 16
DEVICES = PAIRS // ROWS_DEV
CHIPS = DEVICES // 2
WIDE_NARROW = ("wide", "narrow")


def dot_hi(a, b, dims=(((1,), (0,)), ((), ()))):
    return lax.dot_general(a, b, dims, precision=HI, preferred_element_type=F32)

def factor_block(s, at):
    rows = lax.broadcasted_iota(I32, (BLOCK, 2 * BLOCK), 0)
    lanes = lax.broadcasted_iota(I32, (BLOCK, 2 * BLOCK), 1)
    other = BLOCK - at
    inside = (lanes >= at) & (lanes < at + BLOCK)
    t = jnp.where(inside, s, (rows == lanes - other).astype(F32))
    done = []
    c0 = jnp.broadcast_to(t[:, at : at + 1], t.shape)
    c1 = jnp.broadcast_to(t[:, at + 1 : at + 2], t.shape)
    for j in range(0, BLOCK, 2):
        i = j % 8
        r0, r1 = t[i : i + 1, :], t[i + 1 : i + 2, :]
        a, b, c = c0[i : i + 1, :], c0[i + 1 : i + 2, :], c1[i + 1 : i + 2, :]
        inv = 1.0 / (a * c - b * b)
        p, q, s = c * inv, b * inv, a * inv
        ia = 1.0 / a
        done.append(r0 * lax.rsqrt(a))
        done.append((r1 - (b * ia) * r0) * lax.rsqrt(c - b * (b * ia)))
        if j + 2 == BLOCK:
            break
        old = t
        u0 = p * r0 - q * r1
        u1 = s * r1 - q * r0
        below = lax.broadcasted_iota(I32, t.shape, 0) > i + 1
        t = jnp.where(below, t - c0 * u0 - c1 * u1, t)
        nexts = []
        for k in (2, 3):
            x0, x1 = c0[i + k : i + k + 1, :], c1[i + k : i + k + 1, :]
            col = jnp.broadcast_to(old[:, at + j + k : at + j + k + 1], t.shape)
            nexts.append(col - c0 * (p * x0 - q * x1) - c1 * (s * x1 - q * x0))
        c0, c1 = nexts
        if (j + 2) % 8 == 0:
            t, c0, c1 = t[8:, :], c0[8:, :], c1[8:, :]
    full = jnp.concatenate(done, axis=0)
    return full[:, other : other + BLOCK]

def invert_factor(a_ref, w_ref):
    n = a_ref.shape[0]
    w_ref[...] = jnp.zeros_like(w_ref)
    for k in range(0, n, BLOCK):
        e = k + BLOCK
        base = k // 128 * 128
        inv = factor_block(a_ref[k:e, base : base + 128], k - base)
        if k == 0:
            wk = inv
        else:
            wk = jnp.concatenate([dot_hi(inv, w_ref[k:e, :k]), inv], axis=1)
        w_ref[k:e, :e] = wk
        if e < n:
            col = dot_hi(a_ref[e:, k:e], inv, NT)
            a_ref[e:, e:] = a_ref[e:, e:] - dot_hi(col, col, NT)
            w_ref[e:, :e] = w_ref[e:, :e] - dot_hi(col, wk)


def dot_bf(a, b, dims=NN):
    return lax.dot_general(a, b, dims, preferred_element_type=F32)


def bf(x):
    return x.astype(F32).astype(BF16)


def split3(x):
    hi = x.astype(BF16)
    rest = x - hi.astype(F32)
    mid = rest.astype(BF16)
    return hi, mid, (rest - mid.astype(F32)).astype(BF16)


def split2(x):
    hi = x.astype(BF16)
    return hi, (x - hi.astype(F32)).astype(BF16)


def column(row):
    return jnp.broadcast_to(row.astype(F32), (128, row.shape[1])).T.astype(I32)


def own_pivot_integrals(piv, dest, ints_ref, pint_ref):
    piv_col = column(piv)
    match = bf(
        jnp.concatenate([piv_col == dest[:, i : i + 128] for i in range(0, ROWS_DEV, 128)], axis=1)
    )
    rows = sum(dot_bf(match, part) for part in split3(ints_ref[:ROWS_DEV, :]))
    for ct in range(PIVOTS // 128):
        pint_ref[ct * 32 : ct * 32 + 32] = rows[:, ct * 128 : ct * 128 + 128].reshape(32, 8, 128)


def own_pivot_vectors(piv_smem, first, vec_ref, pvec_ref):
    def pick(t, _):
        for u in range(8):
            row = piv_smem[0, t * 8 + u] - first
            mine = (row >= 0) & (row < ROWS_DEV)
            values = vec_ref[pl.ds(jnp.where(mine, row, ROWS_DEV), 1), :]
            for ct in range(VECS // 128):
                pvec_ref[t // 16, ct // 2 * 16 + t % 16, ct % 2, u : u + 1, :] = values[
                    :, ct * 128 : ct * 128 + 128
                ]
        return 0

    lax.fori_loop(0, PIVOTS // 8, pick, 0)


def slot_maps(dest):
    owner = dest // ROWS_DEV
    local1 = dest - owner * ROWS_DEV + 1
    onehot = lax.broadcasted_iota(I32, (DEVICES, ROWS_DEV), 0) == owner
    onehot_bf = bf(onehot)
    before = bf(lax.broadcasted_iota(I32, (128, 128), 0) < lax.broadcasted_iota(I32, (128, 128), 1))
    ranks = []
    carry = jnp.zeros((DEVICES, 1), F32)
    for i in range(0, ROWS_DEV, 128):
        hot = onehot[:, i : i + 128]
        count = dot_bf(onehot_bf[:, i : i + 128], before) + carry
        ranks.append(jnp.sum(jnp.where(hot, count, 0.0), axis=0, keepdims=True))
        carry = carry + jnp.sum(hot.astype(F32), axis=1, keepdims=True)
    rank = jnp.concatenate(ranks, axis=1).astype(I32)
    slot = lax.broadcasted_iota(I32, (CAP, ROWS_DEV), 1)
    hit = lax.broadcasted_iota(I32, (CAP, ROWS_DEV), 0) == rank
    source = dot_bf(bf(jnp.where(hit, slot // 32, 0)), onehot_bf, NT) * 32.0
    source = source + dot_bf(bf(jnp.where(hit, slot % 32, 0)), onehot_bf, NT)
    hit = lax.broadcasted_iota(I32, (128, ROWS_DEV), 0) == rank
    target = dot_bf(onehot_bf, bf(jnp.where(hit, local1 // 32, 0)), NT) * 32.0
    target = target + dot_bf(onehot_bf, bf(jnp.where(hit, local1 % 32, 0)), NT)
    return jnp.clip(source.astype(I32), 0, ROWS_DEV - 1), target.astype(I32)


def row_places(target):
    by_slot = target.astype(F32).T.astype(I32)
    line = lax.broadcasted_iota(I32, (128, DEVICES), 0)
    block = lax.broadcasted_iota(I32, (128, DEVICES), 1)
    highs, blocks, slots = [], [], []
    for k in range(CAP):
        t = by_slot[k : k + 1, :] - 1
        highs.append(bf(line[:32] == t // 32))
        low = line == t % 32
        blocks.append(bf(jnp.where(low, block, 0)))
        slots.append(bf(jnp.where(low, k, 0)))
    high = jnp.concatenate(highs, axis=1)
    place = dot_bf(high, jnp.concatenate(blocks, axis=1), NT) * CAP
    place = place + dot_bf(high, jnp.concatenate(slots, axis=1), NT)
    place = place.astype(I32)
    return place // 8 * 16 + place % 8


def far_first(offsets):
    offsets = list(offsets)
    random.Random(3).shuffle(offsets)
    return sorted(offsets, key=lambda o: -sum(min(v, 4 - v) for v in o[:3]))


CHIP_STEPS = far_first((z, x, y) for z in range(4) for x in range(4) for y in range(4) if (z, x, y) != (0, 0, 0))
PLANE_ORDER = (2, 1, 3, 0)
ROW_SPLIT = (0, 0)
ALL_STEPS = far_first(
    (z, x, y, c)
    for z in range(4) for x in range(4) for y in range(4) for c in range(2)
    if (z, x, y, c) != (0, 0, 0, 0)
)


def main_kernel(
    index_ref, ints_hbm, vec_hbm, out_ref,
    piv_smem, ints_ref, vec_ref, pvec_ref, pint_ref, from_ref, from_smem, send_ref, tgt_ref, rtgt_ref,
    pair_v, pair_i, mine, part, tile, all0, all1, a_ref, w_ref, prod_ref,
    recv_ref, place_ref, place_smem, rows_ref, vh_ref, vl_ref, wh_ref, wl_ref, ssem, rsem, lsem,
):
    wide, narrow = lax.axis_index("wide"), lax.axis_index("narrow")
    z, core, x, y = wide // 2, wide % 2, narrow // 4, narrow % 4
    chip = z * 16 + x * 4 + y
    me = wide * 16 + narrow

    def at(dz, dx, dy, dc=0):
        oz, ox, oy, oc = (z + dz) % 4, (x + dx) % 4, (y + dy) % 4, (core + dc) % 2
        return {"wide": oz * 2 + oc, "narrow": ox * 4 + oy}, oz * 16 + ox * 4 + oy

    def send(src, dst, stage, where):
        pltpu.make_async_remote_copy(
            src_ref=src, dst_ref=dst, send_sem=ssem.at[stage], recv_sem=rsem.at[stage],
            device_id=where, device_id_type=pl.DeviceIdType.MESH,
        ).start()

    def arrived(ref, stage):
        pltpu.make_async_copy(ref, ref, rsem.at[stage]).wait()

    def left(ref, stage):
        pltpu.make_async_copy(ref, ref, ssem.at[stage]).wait()

    load_vec = pltpu.make_async_copy(vec_hbm, vec_ref.at[pl.ds(0, ROWS_DEV)], lsem.at[0])
    load_vec.start()
    load_ints = pltpu.make_async_copy(ints_hbm, ints_ref.at[pl.ds(0, ROWS_DEV)], lsem.at[1])
    load_ints.start()
    load_piv = pltpu.make_async_copy(index_ref.at[:, pl.ds(0, PIVOTS)], piv_smem, lsem.at[3])
    load_piv.start()
    barrier = pltpu.get_barrier_semaphore()
    for step in ALL_STEPS:
        pl.semaphore_signal(barrier, inc=1, device_id=at(*step)[0], device_id_type=pl.DeviceIdType.MESH)
    vec_ref[pl.ds(ROWS_DEV, 8), :] = jnp.zeros((8, VECS), F32)
    dest = index_ref[:, PIVOTS:]
    load_ints.wait()
    own_pivot_integrals(index_ref[:, :PIVOTS], dest, ints_ref, pint_ref)
    load_vec.wait()
    load_piv.wait()
    own_pivot_vectors(piv_smem, me * ROWS_DEV, vec_ref, pvec_ref)
    pl.semaphore_wait(barrier, DEVICES - 1)

    sibling = at(0, 0, 0, 1)[0]
    planes = [pl.ds(pl.multiple_of((z + dz) % 4 * 16, 16), 16) for dz in PLANE_ORDER]
    for n, plane in enumerate(planes):
        send(pvec_ref.at[1 - core, plane], pair_v.at[plane], 10 + n, sibling)

        @pl.when(core == 1)
        def _():
            send(pint_ref.at[plane], pair_i.at[plane], 14 + n, sibling)

    source, target = slot_maps(dest)
    from_ref[...] = source
    tgt_ref[...] = target.reshape(DEVICES, 1, 128)
    to_smem = pltpu.make_async_copy(from_ref, from_smem, lsem.at[2])
    to_smem.start()

    two = pl.ds(0, 2)
    step_slot = {step: i for i, step in enumerate(CHIP_STEPS)}
    for n, plane in enumerate(planes):
        arrived(pair_v.at[plane], 10 + n)
        mine[plane, 0:2] = pvec_ref[core, plane] + pair_v[plane]
        group = [step for step in CHIP_STEPS if step[0] == PLANE_ORDER[n]]

        @pl.when(core == 0)
        def _():
            arrived(pair_i.at[plane], 14 + n)
            mine[plane, 2] = pint_ref[plane] + pair_i[plane]
            for step in group:
                where, home = at(*step)
                send(mine.at[home], part.at[step_slot[step]], 2, where)

        @pl.when(core == 1)
        def _():
            for step in group:
                where, home = at(*step)
                send(mine.at[home, two], part.at[step_slot[step], two], 2, where)

    to_smem.wait()

    def pack(d, _):
        for k in range(CAP):
            row = ints_ref[pl.ds(from_smem[k, d] & (ROWS_DEV - 1), 1), :]
            send_ref[d, pl.ds(k // 8 * 16 + k % 8, 2, 8), :] = jnp.concatenate(
                [row[:, :128], row[:, 128:]], axis=0
            )
        return 0

    lax.fori_loop(0, DEVICES, pack, 0)
    steps = [at(*step)[0] for step in ALL_STEPS]

    def rows_out(begin, end):
        for i in range(begin, end):
            send(
                send_ref.at[steps[i]["wide"] * 16 + steps[i]["narrow"]],
                recv_ref.at[pl.ds(2 * i * CAP, 2 * CAP)], 8, steps[i],
            )

    rows_out(0, ROW_SPLIT[0])
    others = pl.ds(0, CHIPS - 1)

    @pl.when(core == 0)
    def _():
        arrived(part, 2)
        tile[...] = jnp.sum(part[...], axis=0) + mine[chip]
        for step in CHIP_STEPS:
            send(tile, all0.at[chip], 4, at(*step)[0])
        all0[chip] = tile[...]

    @pl.when(core == 1)
    def _():
        arrived(all1.at[others], 2)
        tile[0:2] = jnp.sum(part[:, 0:2], axis=0) + mine[chip, 0:2]
        for step in CHIP_STEPS:
            send(tile.at[two], all1.at[chip], 4, at(*step)[0])
        all1[chip] = tile[0:2]

    for i, where in enumerate(steps):
        send(tgt_ref.at[where["wide"] * 16 + where["narrow"]], rtgt_ref.at[i], 9, where)
    rtgt_ref[DEVICES - 1] = tgt_ref[me]
    rows_out(ROW_SPLIT[0], ROW_SPLIT[1])

    def halve(t, _):
        span = pl.ds(pl.multiple_of(t * 64, 64), 64)
        vh_ref[span, :], vl_ref[span, :] = split2(vec_ref[span, :])
        return 0

    lax.fori_loop(0, ROWS_DEV // 64, halve, 0)
    recv_ref[2 * (DEVICES - 1) * CAP : 2 * DEVICES * CAP, :] = send_ref[me]

    @pl.when(core == 0)
    def _():
        arrived(all0.at[others], 4)
        send(all0, all0, 6, sibling)

    @pl.when(core == 1)
    def _():
        arrived(all1.at[others], 4)
        send(all1, all1, 6, sibling)

    rows_out(ROW_SPLIT[1], DEVICES - 1)

    @pl.when(core == 0)
    def _():
        arrived(all1, 6)

    @pl.when(core == 1)
    def _():
        arrived(all0, 6)

    def pivot_columns(ct):
        top, end = ct * 16, ct * 16 + 16
        return jnp.concatenate(
            [
                jnp.concatenate(
                    [all0[top:end, u].reshape(128, 128), all1[top:end, u].reshape(128, 128)], axis=0
                )
                for u in range(2)
            ],
            axis=1,
        )

    block = jnp.concatenate([all0[u * 32 : u * 32 + 32, 2].reshape(PIVOTS, 128) for u in range(2)], axis=1)
    for ct in range(VECS // 256):
        cols = pivot_columns(ct)
        block = block - dot_hi(cols, cols, NT)
    a_ref[...] = (block + block.T) * 0.5
    invert_factor(a_ref, w_ref)
    wh_ref[...], wl_ref[...] = split2(w_ref[...])
    product = jnp.zeros((ROWS_DEV, PIVOTS), F32)
    for ct in range(VECS // 256):
        span = slice(ct * 256, ct * 256 + 256)
        ph, pl_ = split2(pivot_columns(ct))
        vh = vh_ref[:, span]
        product = product + (dot_bf(vh, ph, NT) + (dot_bf(vh, pl_, NT) + dot_bf(vl_ref[:, span], ph, NT)))
    prod_ref[...] = product
    arrived(rtgt_ref.at[pl.ds(0, DEVICES - 1)], 9)
    place_ref[...] = row_places(rtgt_ref[...].reshape(DEVICES, 128))
    place_copy = pltpu.make_async_copy(place_ref, place_smem, lsem.at[3])
    place_copy.start()
    place_copy.wait()
    arrived(recv_ref.at[pl.ds(0, 2 * (DEVICES - 1) * CAP)], 8)

    def take(q):
        for t in range(CHUNK // 32):
            for u in range(32):
                line = place_smem[q * (CHUNK // 32) + t, u] & (2 * DEVICES * CAP - 9)
                rows_ref[t * 4 + u // 8, pl.ds(u % 8, 2, 8), :] = recv_ref[pl.ds(line, 2, 8), :]

    def finish(q, rows):
        span = pl.ds(pl.multiple_of(q * CHUNK, CHUNK), CHUNK)
        rh, rl = split2(rows - prod_ref[span, :])
        wh = wh_ref[...]
        out_ref[span, :] = dot_bf(rh, wh, NT) + (dot_bf(rh, wl_ref[...], NT) + dot_bf(rl, wh, NT))

    def gathered():
        return jnp.concatenate([rows_ref[: CHUNK // 8, h * 8 : h * 8 + 8].reshape(CHUNK, 128) for h in range(2)], axis=1)

    def step(q, _):
        rows = gathered()
        take(q + 1)
        finish(q, rows)
        return 0

    take(0)
    lax.fori_loop(0, ROWS_DEV // CHUNK - 1, step, 0)
    finish(ROWS_DEV // CHUNK - 1, gathered())

    for n, plane in enumerate(planes):
        left(pair_v.at[plane], 10 + n)
    left(recv_ref.at[pl.ds(0, 2 * (DEVICES - 1) * CAP)], 8)
    left(rtgt_ref.at[pl.ds(0, DEVICES - 1)], 9)

    @pl.when(core == 0)
    def _():
        left(part, 2)
        left(all0.at[others], 4)
        left(all0, 6)

    @pl.when(core == 1)
    def _():
        for n, plane in enumerate(planes):
            left(pair_i.at[plane], 14 + n)
        left(all1.at[others], 2)
        left(all1.at[others], 4)
        left(all1, 6)


VMEM_LIMIT = 52 << 20
CHUNK = 256


def exchange(vectors, pivots, integrals, destination):
    vmem = pl.BlockSpec(memory_space=pltpu.VMEM)
    hbm = pl.BlockSpec(memory_space=pltpu.HBM)
    return pl.pallas_call(
        main_kernel,
        out_shape=jax.ShapeDtypeStruct((ROWS_DEV, PIVOTS), F32),
        in_specs=[vmem, hbm, hbm],
        out_specs=vmem,
        scratch_shapes=[
            pltpu.SMEM((1, PIVOTS), I32),
            pltpu.VMEM((ROWS_DEV + 32, PIVOTS), F32),
            pltpu.VMEM((ROWS_DEV + 8, VECS), F32),
            pltpu.VMEM((3, CHIPS, 2, 8, 128), F32),
            pltpu.VMEM((CHIPS, 8, 128), F32),
            pltpu.VMEM((CAP, DEVICES), I32),
            pltpu.SMEM((CAP, DEVICES), I32),
            pltpu.VMEM((DEVICES + 2, 2 * CAP, 128), F32),
            pltpu.VMEM((DEVICES, 1, 128), I32),
            pltpu.VMEM((DEVICES, 1, 128), I32),
            pltpu.VMEM((CHIPS, 2, 8, 128), F32),
            pltpu.VMEM((CHIPS, 8, 128), F32),
            pltpu.VMEM((CHIPS, 3, 8, 128), F32),
            pltpu.VMEM((CHIPS - 1, 3, 8, 128), F32),
            pltpu.VMEM((3, 8, 128), F32),
            pltpu.VMEM((CHIPS, 3, 8, 128), F32),
            pltpu.VMEM((CHIPS, 2, 8, 128), F32),
            pltpu.VMEM((PIVOTS, PIVOTS), F32),
            pltpu.VMEM((PIVOTS, PIVOTS), F32),
            pltpu.VMEM((ROWS_DEV, PIVOTS), F32),
            pltpu.VMEM((2 * DEVICES * CAP + 64, 128), F32),
            pltpu.VMEM((32, 128), I32),
            pltpu.SMEM((32, 128), I32),
            pltpu.VMEM((CHUNK // 8 + 4, 16, 128), F32),
            pltpu.VMEM((ROWS_DEV, VECS), BF16),
            pltpu.VMEM((ROWS_DEV, VECS), BF16),
            pltpu.VMEM((PIVOTS, PIVOTS), BF16),
            pltpu.VMEM((PIVOTS, PIVOTS), BF16),
            pltpu.SemaphoreType.DMA((18,)),
            pltpu.SemaphoreType.DMA((18,)),
            pltpu.SemaphoreType.DMA((4,)),
        ],
        compiler_params=pltpu.CompilerParams(
            collective_id=0, has_side_effects=True, vmem_limit_bytes=VMEM_LIMIT
        ),
        name="exchange",
    )(jnp.concatenate([pivots, destination]).reshape(1, -1), integrals, vectors)


def solution(mesh):
    return jax.shard_map(
        exchange,
        mesh=mesh,
        in_specs=(P(WIDE_NARROW, None), P(), P(WIDE_NARROW, None), P(WIDE_NARROW)),
        out_specs=P(WIDE_NARROW, None),
        check_vma=False,
    )
```

```python
import random

import jax, jax.numpy as jnp
from jax import lax
from jax.experimental import pallas as pl
from jax.experimental.pallas import tpu as pltpu
from jax.sharding import PartitionSpec as P

F32, BF16, I32 = jnp.float32, jnp.bfloat16, jnp.int32
HI = lax.Precision.HIGHEST
NT = (((1,), (1,)), ((), ()))
NN = (((1,), (0,)), ((), ()))
TN = (((0,), (0,)), ((), ()))
BLOCK = 64
PAIRS = 131072
ROWS_DEV = 1024
VECS = 1024
PIVOTS = 256
CAP = 16
DEVICES = PAIRS // ROWS_DEV
CHIPS = DEVICES // 2
WIDE_NARROW = ("wide", "narrow")


def dot_hi(a, b, dims=(((1,), (0,)), ((), ()))):
    return lax.dot_general(a, b, dims, precision=HI, preferred_element_type=F32)

def factor_block(s, at):
    rows = lax.broadcasted_iota(I32, (BLOCK, 2 * BLOCK), 0)
    lanes = lax.broadcasted_iota(I32, (BLOCK, 2 * BLOCK), 1)
    other = BLOCK - at
    inside = (lanes >= at) & (lanes < at + BLOCK)
    t = jnp.where(inside, s, (rows == lanes - other).astype(F32))
    done = []
    c0 = jnp.broadcast_to(t[:, at : at + 1], t.shape)
    c1 = jnp.broadcast_to(t[:, at + 1 : at + 2], t.shape)
    for j in range(0, BLOCK, 2):
        i = j % 8
        r0, r1 = t[i : i + 1, :], t[i + 1 : i + 2, :]
        a, b, c = c0[i : i + 1, :], c0[i + 1 : i + 2, :], c1[i + 1 : i + 2, :]
        inv = 1.0 / (a * c - b * b)
        p, q, s = c * inv, b * inv, a * inv
        ia = 1.0 / a
        done.append(r0 * lax.rsqrt(a))
        done.append((r1 - (b * ia) * r0) * lax.rsqrt(c - b * (b * ia)))
        if j + 2 == BLOCK:
            break
        old = t
        u0 = p * r0 - q * r1
        u1 = s * r1 - q * r0
        below = lax.broadcasted_iota(I32, t.shape, 0) > i + 1
        t = jnp.where(below, t - c0 * u0 - c1 * u1, t)
        nexts = []
        for k in (2, 3):
            x0, x1 = c0[i + k : i + k + 1, :], c1[i + k : i + k + 1, :]
            col = jnp.broadcast_to(old[:, at + j + k : at + j + k + 1], t.shape)
            nexts.append(col - c0 * (p * x0 - q * x1) - c1 * (s * x1 - q * x0))
        c0, c1 = nexts
        if (j + 2) % 8 == 0:
            t, c0, c1 = t[8:, :], c0[8:, :], c1[8:, :]
    full = jnp.concatenate(done, axis=0)
    return full[:, other : other + BLOCK]

def invert_factor(a_ref, w_ref):
    n = a_ref.shape[0]
    w_ref[...] = jnp.zeros_like(w_ref)
    for k in range(0, n, BLOCK):
        e = k + BLOCK
        base = k // 128 * 128
        inv = factor_block(a_ref[k:e, base : base + 128], k - base)
        if k == 0:
            wk = inv
        else:
            wk = jnp.concatenate([dot_hi(inv, w_ref[k:e, :k]), inv], axis=1)
        w_ref[k:e, :e] = wk
        if e < n:
            col = dot_hi(a_ref[e:, k:e], inv, NT)
            a_ref[e:, e:] = a_ref[e:, e:] - dot_hi(col, col, NT)
            w_ref[e:, :e] = w_ref[e:, :e] - dot_hi(col, wk)


def dot_bf(a, b, dims=NN):
    return lax.dot_general(a, b, dims, preferred_element_type=F32)


def bf(x):
    return x.astype(F32).astype(BF16)


def split3(x):
    hi = x.astype(BF16)
    rest = x - hi.astype(F32)
    mid = rest.astype(BF16)
    return hi, mid, (rest - mid.astype(F32)).astype(BF16)


def split2(x):
    hi = x.astype(BF16)
    return hi, (x - hi.astype(F32)).astype(BF16)


def column(row):
    return jnp.broadcast_to(row.astype(F32), (128, row.shape[1])).T.astype(I32)


def own_pivot_integrals(piv, dest, ints_ref, pint_ref):
    piv_col = column(piv)
    match = bf(
        jnp.concatenate([piv_col == dest[:, i : i + 128] for i in range(0, ROWS_DEV, 128)], axis=1)
    )
    rows = sum(dot_bf(match, part) for part in split3(ints_ref[:ROWS_DEV, :]))
    for ct in range(PIVOTS // 128):
        pint_ref[ct * 32 : ct * 32 + 32] = rows[:, ct * 128 : ct * 128 + 128].reshape(32, 8, 128)


def own_pivot_vectors(piv_smem, first, vec_ref, pvec_ref):
    def pick(t, _):
        for u in range(8):
            row = piv_smem[0, t * 8 + u] - first
            mine = (row >= 0) & (row < ROWS_DEV)
            values = vec_ref[pl.ds(jnp.where(mine, row, ROWS_DEV), 1), :]
            for ct in range(VECS // 128):
                pvec_ref[t // 16, ct // 2 * 16 + t % 16, ct % 2, u : u + 1, :] = values[
                    :, ct * 128 : ct * 128 + 128
                ]
        return 0

    lax.fori_loop(0, PIVOTS // 8, pick, 0)


def slot_maps(dest):
    owner = dest // ROWS_DEV
    local1 = dest - owner * ROWS_DEV + 1
    onehot = lax.broadcasted_iota(I32, (DEVICES, ROWS_DEV), 0) == owner
    onehot_bf = bf(onehot)
    before = bf(lax.broadcasted_iota(I32, (128, 128), 0) < lax.broadcasted_iota(I32, (128, 128), 1))
    ranks = []
    carry = jnp.zeros((DEVICES, 1), F32)
    for i in range(0, ROWS_DEV, 128):
        hot = onehot[:, i : i + 128]
        count = dot_bf(onehot_bf[:, i : i + 128], before) + carry
        ranks.append(jnp.sum(jnp.where(hot, count, 0.0), axis=0, keepdims=True))
        carry = carry + jnp.sum(hot.astype(F32), axis=1, keepdims=True)
    rank = jnp.concatenate(ranks, axis=1).astype(I32)
    slot = lax.broadcasted_iota(I32, (CAP, ROWS_DEV), 1)
    hit = lax.broadcasted_iota(I32, (CAP, ROWS_DEV), 0) == rank
    source = dot_bf(bf(jnp.where(hit, slot // 32, 0)), onehot_bf, NT) * 32.0
    source = source + dot_bf(bf(jnp.where(hit, slot % 32, 0)), onehot_bf, NT)
    hit = lax.broadcasted_iota(I32, (128, ROWS_DEV), 0) == rank
    target = dot_bf(onehot_bf, bf(jnp.where(hit, local1 // 32, 0)), NT) * 32.0
    target = target + dot_bf(onehot_bf, bf(jnp.where(hit, local1 % 32, 0)), NT)
    return jnp.clip(source.astype(I32), 0, ROWS_DEV - 1), target.astype(I32)


def row_places(target):
    by_slot = target.astype(F32).T.astype(I32)
    line = lax.broadcasted_iota(I32, (128, DEVICES), 0)
    block = lax.broadcasted_iota(I32, (128, DEVICES), 1)
    highs, blocks, slots = [], [], []
    for k in range(CAP):
        t = by_slot[k : k + 1, :] - 1
        highs.append(bf(line[:32] == t // 32))
        low = line == t % 32
        blocks.append(bf(jnp.where(low, block, 0)))
        slots.append(bf(jnp.where(low, k, 0)))
    high = jnp.concatenate(highs, axis=1)
    place = dot_bf(high, jnp.concatenate(blocks, axis=1), NT) * CAP
    place = place + dot_bf(high, jnp.concatenate(slots, axis=1), NT)
    place = jnp.clip(place.astype(I32), 0, DEVICES * CAP - 1)
    return place // 8 * 16 + place % 8


def far_first(offsets):
    offsets = list(offsets)
    random.Random(3).shuffle(offsets)
    return sorted(offsets, key=lambda o: -sum(min(v, 4 - v) for v in o[:3]))


CHIP_STEPS = far_first((z, x, y) for z in range(4) for x in range(4) for y in range(4) if (z, x, y) != (0, 0, 0))
PLANE_ORDER = (2, 1, 3, 0)
ROW_SPLIT = (0, 0)
ALL_STEPS = far_first(
    (z, x, y, c)
    for z in range(4) for x in range(4) for y in range(4) for c in range(2)
    if (z, x, y, c) != (0, 0, 0, 0)
)


def main_kernel(
    index_ref, ints_hbm, vec_hbm, out_ref,
    piv_smem, ints_ref, vec_ref, pvec_ref, pint_ref, from_ref, from_smem, send_ref, tgt_ref, rtgt_ref,
    pair_v, pair_i, mine, part, tile, all0, all1, a_ref, w_ref, prod_ref,
    recv_ref, place_ref, place_smem, rows_ref, vh_ref, vl_ref, wh_ref, wl_ref, ssem, rsem, lsem,
):
    wide, narrow = lax.axis_index("wide"), lax.axis_index("narrow")
    z, core, x, y = wide // 2, wide % 2, narrow // 4, narrow % 4
    chip = z * 16 + x * 4 + y
    me = wide * 16 + narrow

    def at(dz, dx, dy, dc=0):
        oz, ox, oy, oc = (z + dz) % 4, (x + dx) % 4, (y + dy) % 4, (core + dc) % 2
        return {"wide": oz * 2 + oc, "narrow": ox * 4 + oy}, oz * 16 + ox * 4 + oy

    def send(src, dst, stage, where):
        pltpu.make_async_remote_copy(
            src_ref=src, dst_ref=dst, send_sem=ssem.at[stage], recv_sem=rsem.at[stage],
            device_id=where, device_id_type=pl.DeviceIdType.MESH,
        ).start()

    def arrived(ref, stage):
        pltpu.make_async_copy(ref, ref, rsem.at[stage]).wait()

    def left(ref, stage):
        pltpu.make_async_copy(ref, ref, ssem.at[stage]).wait()

    load_vec = pltpu.make_async_copy(vec_hbm, vec_ref.at[pl.ds(0, ROWS_DEV)], lsem.at[0])
    load_vec.start()
    load_ints = pltpu.make_async_copy(ints_hbm, ints_ref.at[pl.ds(0, ROWS_DEV)], lsem.at[1])
    load_ints.start()
    load_piv = pltpu.make_async_copy(index_ref.at[:, pl.ds(0, PIVOTS)], piv_smem, lsem.at[3])
    load_piv.start()
    barrier = pltpu.get_barrier_semaphore()
    for step in ALL_STEPS:
        pl.semaphore_signal(barrier, inc=1, device_id=at(*step)[0], device_id_type=pl.DeviceIdType.MESH)
    vec_ref[pl.ds(ROWS_DEV, 8), :] = jnp.zeros((8, VECS), F32)
    dest = index_ref[:, PIVOTS:]
    load_ints.wait()
    own_pivot_integrals(index_ref[:, :PIVOTS], dest, ints_ref, pint_ref)
    load_vec.wait()
    load_piv.wait()
    own_pivot_vectors(piv_smem, me * ROWS_DEV, vec_ref, pvec_ref)
    pl.semaphore_wait(barrier, DEVICES - 1)

    sibling = at(0, 0, 0, 1)[0]
    planes = [pl.ds(pl.multiple_of((z + dz) % 4 * 16, 16), 16) for dz in PLANE_ORDER]
    for n, plane in enumerate(planes):
        send(pvec_ref.at[1 - core, plane], pair_v.at[plane], 10 + n, sibling)

        @pl.when(core == 1)
        def _():
            send(pint_ref.at[plane], pair_i.at[plane], 14 + n, sibling)

    source, target = slot_maps(dest)
    from_ref[...] = source
    tgt_ref[...] = target.reshape(DEVICES, 1, 128)
    to_smem = pltpu.make_async_copy(from_ref, from_smem, lsem.at[2])
    to_smem.start()

    two = pl.ds(0, 2)
    step_slot = {step: i for i, step in enumerate(CHIP_STEPS)}
    for n, plane in enumerate(planes):
        arrived(pair_v.at[plane], 10 + n)
        mine[plane, 0:2] = pvec_ref[core, plane] + pair_v[plane]
        group = [step for step in CHIP_STEPS if step[0] == PLANE_ORDER[n]]

        @pl.when(core == 0)
        def _():
            arrived(pair_i.at[plane], 14 + n)
            mine[plane, 2] = pint_ref[plane] + pair_i[plane]
            for step in group:
                where, home = at(*step)
                send(mine.at[home], part.at[step_slot[step]], 2, where)

        @pl.when(core == 1)
        def _():
            for step in group:
                where, home = at(*step)
                send(mine.at[home, two], part.at[step_slot[step], two], 2, where)

    to_smem.wait()

    def pack(d, _):
        for k in range(CAP):
            row = ints_ref[pl.ds(from_smem[k, d] & (ROWS_DEV - 1), 1), :]
            send_ref[d, pl.ds(k // 8 * 16 + k % 8, 2, 8), :] = jnp.concatenate(
                [row[:, :128], row[:, 128:]], axis=0
            )
        return 0

    lax.fori_loop(0, DEVICES, pack, 0)
    steps = [at(*step)[0] for step in ALL_STEPS]

    def rows_out(begin, end):
        for i in range(begin, end):
            send(
                send_ref.at[steps[i]["wide"] * 16 + steps[i]["narrow"]],
                recv_ref.at[pl.ds(2 * i * CAP, 2 * CAP)], 8, steps[i],
            )

    rows_out(0, ROW_SPLIT[0])
    others = pl.ds(0, CHIPS - 1)

    @pl.when(core == 0)
    def _():
        arrived(part, 2)
        tile[...] = jnp.sum(part[...], axis=0) + mine[chip]
        for step in CHIP_STEPS:
            send(tile, all0.at[chip], 4, at(*step)[0])
        all0[chip] = tile[...]

    @pl.when(core == 1)
    def _():
        arrived(all1.at[others], 2)
        tile[0:2] = jnp.sum(part[:, 0:2], axis=0) + mine[chip, 0:2]
        for step in CHIP_STEPS:
            send(tile.at[two], all1.at[chip], 4, at(*step)[0])
        all1[chip] = tile[0:2]

    for i, where in enumerate(steps):
        send(tgt_ref.at[where["wide"] * 16 + where["narrow"]], rtgt_ref.at[i], 9, where)
    rtgt_ref[DEVICES - 1] = tgt_ref[me]
    rows_out(ROW_SPLIT[0], ROW_SPLIT[1])

    def halve(t, _):
        span = pl.ds(pl.multiple_of(t * 64, 64), 64)
        vh_ref[span, :], vl_ref[span, :] = split2(vec_ref[span, :])
        return 0

    lax.fori_loop(0, ROWS_DEV // 64, halve, 0)
    recv_ref[2 * (DEVICES - 1) * CAP : 2 * DEVICES * CAP, :] = send_ref[me]

    @pl.when(core == 0)
    def _():
        arrived(all0.at[others], 4)
        send(all0, all0, 6, sibling)

    @pl.when(core == 1)
    def _():
        arrived(all1.at[others], 4)
        send(all1, all1, 6, sibling)

    rows_out(ROW_SPLIT[1], DEVICES - 1)

    @pl.when(core == 0)
    def _():
        arrived(all1, 6)

    @pl.when(core == 1)
    def _():
        arrived(all0, 6)

    def pivot_columns(ct):
        top, end = ct * 16, ct * 16 + 16
        return jnp.concatenate(
            [
                jnp.concatenate(
                    [all0[top:end, u].reshape(128, 128), all1[top:end, u].reshape(128, 128)], axis=0
                )
                for u in range(2)
            ],
            axis=1,
        )

    block = jnp.concatenate([all0[u * 32 : u * 32 + 32, 2].reshape(PIVOTS, 128) for u in range(2)], axis=1)
    for ct in range(VECS // 256):
        cols = pivot_columns(ct)
        block = block - dot_hi(cols, cols, NT)
    a_ref[...] = (block + block.T) * 0.5
    invert_factor(a_ref, w_ref)
    wh_ref[...], wl_ref[...] = split2(w_ref[...])
    product = jnp.zeros((ROWS_DEV, PIVOTS), F32)
    for ct in range(VECS // 256):
        span = slice(ct * 256, ct * 256 + 256)
        ph, pl_ = split2(pivot_columns(ct))
        vh = vh_ref[:, span]
        product = product + (dot_bf(vh, ph, NT) + (dot_bf(vh, pl_, NT) + dot_bf(vl_ref[:, span], ph, NT)))
    prod_ref[...] = product
    arrived(rtgt_ref.at[pl.ds(0, DEVICES - 1)], 9)
    place_ref[...] = row_places(rtgt_ref[...].reshape(DEVICES, 128))
    place_copy = pltpu.make_async_copy(place_ref, place_smem, lsem.at[3])
    place_copy.start()
    place_copy.wait()
    arrived(recv_ref.at[pl.ds(0, 2 * (DEVICES - 1) * CAP)], 8)

    def take(q):
        for t in range(CHUNK // 32):
            for u in range(32):
                line = place_smem[q * (CHUNK // 32) + t, u]
                rows_ref[t * 4 + u // 8, pl.ds(u % 8, 2, 8), :] = recv_ref[pl.ds(line, 2, 8), :]

    def finish(q, rows):
        span = pl.ds(pl.multiple_of(q * CHUNK, CHUNK), CHUNK)
        rh, rl = split2(rows - prod_ref[span, :])
        wh = wh_ref[...]
        out_ref[span, :] = dot_bf(rh, wh, NT) + (dot_bf(rh, wl_ref[...], NT) + dot_bf(rl, wh, NT))

    def gathered():
        return jnp.concatenate([rows_ref[: CHUNK // 8, h * 8 : h * 8 + 8].reshape(CHUNK, 128) for h in range(2)], axis=1)

    def step(q, _):
        rows = gathered()
        take(q + 1)
        finish(q, rows)
        return 0

    take(0)
    lax.fori_loop(0, ROWS_DEV // CHUNK - 1, step, 0)
    finish(ROWS_DEV // CHUNK - 1, gathered())

    for n, plane in enumerate(planes):
        left(pair_v.at[plane], 10 + n)
    left(recv_ref.at[pl.ds(0, 2 * (DEVICES - 1) * CAP)], 8)
    left(rtgt_ref.at[pl.ds(0, DEVICES - 1)], 9)

    @pl.when(core == 0)
    def _():
        left(part, 2)
        left(all0.at[others], 4)
        left(all0, 6)

    @pl.when(core == 1)
    def _():
        for n, plane in enumerate(planes):
            left(pair_i.at[plane], 14 + n)
        left(all1.at[others], 2)
        left(all1.at[others], 4)
        left(all1, 6)


VMEM_LIMIT = 52 << 20
CHUNK = 256


def exchange(vectors, pivots, integrals, destination):
    vmem = pl.BlockSpec(memory_space=pltpu.VMEM)
    hbm = pl.BlockSpec(memory_space=pltpu.HBM)
    return pl.pallas_call(
        main_kernel,
        out_shape=jax.ShapeDtypeStruct((ROWS_DEV, PIVOTS), F32),
        in_specs=[vmem, hbm, hbm],
        out_specs=vmem,
        scratch_shapes=[
            pltpu.SMEM((1, PIVOTS), I32),
            pltpu.VMEM((ROWS_DEV + 32, PIVOTS), F32),
            pltpu.VMEM((ROWS_DEV + 8, VECS), F32),
            pltpu.VMEM((3, CHIPS, 2, 8, 128), F32),
            pltpu.VMEM((CHIPS, 8, 128), F32),
            pltpu.VMEM((CAP, DEVICES), I32),
            pltpu.SMEM((CAP, DEVICES), I32),
            pltpu.VMEM((DEVICES + 2, 2 * CAP, 128), F32),
            pltpu.VMEM((DEVICES, 1, 128), I32),
            pltpu.VMEM((DEVICES, 1, 128), I32),
            pltpu.VMEM((CHIPS, 2, 8, 128), F32),
            pltpu.VMEM((CHIPS, 8, 128), F32),
            pltpu.VMEM((CHIPS, 3, 8, 128), F32),
            pltpu.VMEM((CHIPS - 1, 3, 8, 128), F32),
            pltpu.VMEM((3, 8, 128), F32),
            pltpu.VMEM((CHIPS, 3, 8, 128), F32),
            pltpu.VMEM((CHIPS, 2, 8, 128), F32),
            pltpu.VMEM((PIVOTS, PIVOTS), F32),
            pltpu.VMEM((PIVOTS, PIVOTS), F32),
            pltpu.VMEM((ROWS_DEV, PIVOTS), F32),
            pltpu.VMEM((2 * DEVICES * CAP + 64, 128), F32),
            pltpu.VMEM((32, 128), I32),
            pltpu.SMEM((32, 128), I32),
            pltpu.VMEM((CHUNK // 8 + 4, 16, 128), F32),
            pltpu.VMEM((ROWS_DEV, VECS), BF16),
            pltpu.VMEM((ROWS_DEV, VECS), BF16),
            pltpu.VMEM((PIVOTS, PIVOTS), BF16),
            pltpu.VMEM((PIVOTS, PIVOTS), BF16),
            pltpu.SemaphoreType.DMA((18,)),
            pltpu.SemaphoreType.DMA((18,)),
            pltpu.SemaphoreType.DMA((4,)),
        ],
        compiler_params=pltpu.CompilerParams(
            collective_id=0, has_side_effects=True, vmem_limit_bytes=VMEM_LIMIT
        ),
        name="exchange",
    )(jnp.concatenate([pivots, destination]).reshape(1, -1), integrals, vectors)


def solution(mesh):
    return jax.shard_map(
        exchange,
        mesh=mesh,
        in_specs=(P(WIDE_NARROW, None), P(), P(WIDE_NARROW, None), P(WIDE_NARROW)),
        out_specs=P(WIDE_NARROW, None),
        check_vma=False,
    )
```
